128 devices in a mesh: section: 8 (over x_lo, y), dp: 16 (over z, x_hi, core).
Axes of the slice: x: 4 (x_hi: 2, x_lo: 2; x = x_hi * 2 + x_lo), y: 4, z: 4, core: 2. Of those that a mesh axis runs over, the one named last changes fastest.
Arguments:
- acts: bfloat16 [8, 256, 196, 1024], P('section', 'dp'), may hold values from -8 to 8, as said below
- patches: bfloat16 [256, 196, 768], P('dp', None, 'section'), may hold values from -6 to 6
- labels: int32 [256], P('dp'), may hold values from 0 to 11263
- w_first: bfloat16 [8, 1024, 256], P('section'), may hold values from -0.1875 to 0.1875
- w_second: bfloat16 [8, 256, 1024], P('section'), may hold values from -0.375 to 0.375
- w_decode: bfloat16 [8, 1024, 768], P('section'), may hold values from -0.1875 to 0.1875
- w_aux: bfloat16 [8, 1024, 512], P('section'), may hold values from -0.1875 to 0.1875
- w_class: bfloat16 [8, 11264, 512], P('section', 'dp'), may hold values from -1.5 to 1.5
Outputs:
- grad_first: float32 [8, 1024, 256], P('section', 'dp')
- grad_second: float32 [8, 256, 1024], P('section', 'dp')
- grad_decode: float32 [8, 1024, 768], P('section', 'dp')
- grad_aux: float32 [8, 1024, 512], P('section', 'dp')
- grad_class: float32 [8, 11264, 512], P('section', 'dp')
The draws below stay inside these ranges and needn't reach their ends.
Inputs may be any that keep to these rules, and one draw needn't show every extreme that they name: `acts`: feature maps with a per-image, per-channel offset.
All inputs are finite; a program needn't handle non-finite values.
Results may differ from the reference program's by a relative error of at most 0.03.
The reference program's roundings to bfloat16 on the way count: a program that leaves them out, or rounds other values in their place, can miss the bound.
Values may be sent and summed in bfloat16 or wider, within the bound.
A program may use at most 192 MiB of HBM per device.

```python
import jax
import jax.numpy as jnp
from jax import lax

C = 1024
BOT = 256
PIX = 196
PATCH = 768
HEAD = 512
CLASSES = 11264
MODULES = 8
IMAGES = 256
ROWS = 50176
N_DP = 16


def draw_acts(key, part):
    key_base = jax.random.fold_in(key, 11)
    key_offset = jax.random.fold_in(key, 12)
    shape = (MODULES, IMAGES, PIX, C)
    base = jax.random.normal(key_base, shape, jnp.float32)
    offset = jax.random.normal(key_offset, (MODULES, IMAGES, 1, C), jnp.float32)
    values = 0.7 * base + offset
    return jnp.clip(values, -8.0, 8.0).astype(jnp.bfloat16)


def draw_w_class(key, part):
    key_base = jax.random.fold_in(key, 21)
    shape = (MODULES, CLASSES, HEAD)
    values = 0.18 * jax.random.normal(key_base, shape, jnp.float32)
    return jnp.clip(values, -1.5, 1.5).astype(jnp.bfloat16)


def plant(values, key, least, high):
    spot = [jax.random.randint(jax.random.fold_in(key, axis), (), 0, length) for axis, length in enumerate(values.shape)]
    main_axis = values.shape.index(max(values.shape))
    neighbour = spot[:main_axis] + [(spot[main_axis] + 1) % values.shape[main_axis]] + spot[main_axis + 1:]
    return values.at[tuple(spot)].set(least).at[tuple(neighbour)].set(high)


def shard_levels(key, shape, split, low, top_value):
    level, own = 1.0, jax.random.fold_in(key, 6)
    for dim, blocks in split:
        draws = jnp.exp(jax.random.uniform(jax.random.fold_in(own, dim), (blocks,), jnp.float32, low / len(split), top_value / len(split)))
        level = level * jnp.repeat(draws, shape[dim] // blocks).reshape([-1 if axis == dim else 1 for axis in range(len(shape))])
    return level


def centred(stream_key, extent, scale, reach, shards=(), kind=jnp.bfloat16):
    factor_of = shard_levels(stream_key, extent, shards, -0.22, 0.18) if shards else 1.0
    values = jax.random.normal(stream_key, extent, jnp.float32) * scale * factor_of
    return jnp.minimum(jnp.maximum(values, -reach), reach).astype(kind)


def setup_inputs(seed: int = 0) -> dict:
    streams_of = jax.random.split(jax.random.key(seed), 9)
    acts = draw_acts(jax.random.fold_in(streams_of[8], 71), 0)
    patches = centred(streams_of[1], (IMAGES, PIX, PATCH), 1.0, 6.0, ((0, 16), (2, 8)))
    labels = plant(jax.random.randint(streams_of[2], (IMAGES,), 0, CLASSES), jax.random.fold_in(streams_of[2], 1), 0, CLASSES - 1).astype(jnp.int32)
    w_first = centred(streams_of[3], (MODULES, C, BOT), C ** -0.5, 0.1875, ((0, 8),))
    w_second = centred(streams_of[4], (MODULES, BOT, C), BOT ** -0.5, 0.375, ((0, 8),))
    w_decode = centred(streams_of[5], (MODULES, C, PATCH), C ** -0.5, 0.1875, ((0, 8),))
    w_aux = centred(streams_of[6], (MODULES, C, HEAD), C ** -0.5, 0.1875, ((0, 8),))
    w_class = draw_w_class(jax.random.fold_in(streams_of[8], 71), 0)
    return dict(acts=acts, patches=patches, labels=labels, w_first=w_first, w_second=w_second, w_decode=w_decode, w_aux=w_aux, w_class=w_class)


def block_sum(left, right):
    lb = left.reshape(N_DP, -1, left.shape[1]).astype(jnp.float32)
    rb = right.reshape(N_DP, -1, right.shape[1]).astype(jnp.float32)
    parts = jnp.einsum("kra,krb->kab", lb, rb)
    parts = lax.optimization_barrier(parts.astype(jnp.bfloat16))
    return jnp.sum(parts.astype(jnp.float32), axis=0)


def one_module(items):
    acts_m, patches, labels, first, second, decode, aux, klass = items
    flat = acts_m.reshape(ROWS, C)
    pre_act = jnp.dot(flat, first, preferred_element_type=jnp.float32)
    hidden = jax.nn.relu(pre_act).astype(jnp.bfloat16)
    feature = (flat.astype(jnp.float32) + jnp.dot(hidden, second, preferred_element_type=jnp.float32)).astype(jnp.bfloat16)
    recon = jnp.dot(feature, decode, preferred_element_type=jnp.float32)
    target = patches.reshape(ROWS, PATCH).astype(jnp.float32)
    recon_grad = ((recon - target) / (ROWS ** 0.5)).astype(jnp.bfloat16)
    pooled = jnp.mean(feature.reshape(IMAGES, PIX, C).astype(jnp.float32), axis=1).astype(jnp.bfloat16)
    aux_pre = jnp.dot(pooled, aux, preferred_element_type=jnp.float32)
    aux_out = jax.nn.relu(aux_pre).astype(jnp.bfloat16)
    logits = jnp.dot(aux_out, klass.T, preferred_element_type=jnp.float32)
    top = jnp.max(logits, axis=1, keepdims=True)
    expo = jnp.exp(logits - top)
    prob = expo / jnp.sum(expo, axis=1, keepdims=True)
    onehot = (labels[:, None] == jnp.arange(CLASSES, dtype=jnp.int32)[None, :]).astype(jnp.float32)
    logit_grad = ((prob - onehot) / (IMAGES ** 0.5)).astype(jnp.bfloat16)
    grad_class = jnp.dot(logit_grad.T, aux_out, preferred_element_type=jnp.float32)
    back = jnp.dot(logit_grad, klass, preferred_element_type=jnp.float32)
    aux_grad = jnp.where(aux_pre > 0, back, 0.0).astype(jnp.bfloat16)
    pooled_grad = jnp.dot(aux_grad, aux.T, preferred_element_type=jnp.float32)
    dec_back = jnp.dot(recon_grad, decode.T, preferred_element_type=jnp.float32)
    feature_grad = (dec_back.reshape(IMAGES, PIX, C) + pooled_grad[:, None, :] / PIX).reshape(ROWS, C).astype(jnp.bfloat16)
    hid_back = jnp.dot(feature_grad, second.T, preferred_element_type=jnp.float32)
    hidden_grad = jnp.where(pre_act > 0, hid_back, 0.0).astype(jnp.bfloat16)
    grad_first = block_sum(flat, hidden_grad)
    grad_second = block_sum(hidden, feature_grad)
    grad_decode = block_sum(feature, recon_grad)
    grad_aux = block_sum(pooled, aux_grad)
    return grad_first, grad_second, grad_decode, grad_aux, grad_class


def reference(acts, patches, labels, w_first, w_second, w_decode, w_aux, w_class):
    results = []
    for module in range(MODULES):
        results.append(one_module((acts[module], patches, labels, w_first[module], w_second[module], w_decode[module], w_aux[module], w_class[module])))
    return (jnp.stack([r[0] for r in results]), jnp.stack([r[1] for r in results]), jnp.stack([r[2] for r in results]), jnp.stack([r[3] for r in results]), jnp.stack([r[4] for r in results]))
```

```python
import functools

import jax
import jax.numpy as jnp
from jax import lax
from jax.experimental import pallas as pl
from jax.experimental.pallas import tpu as pltpu
from jax.sharding import PartitionSpec as P

MESH = pl.DeviceIdType.MESH
F32 = jnp.float32
BF16 = jnp.bfloat16

C = 1024
BOT = 256
PIX = 196
PAD = 208
PATCH = 768
HEAD = 512
CLASSES = 11264
SEC = 8
DP = 16
IMG = 16
CHUNKS = 4
PER = IMG // CHUNKS
CROWS = PER * PAD
SLICE = PATCH // SEC
PROWS = 3 * PAD
CSHARD = CLASSES // DP


def dot(a, b):
    return lax.dot_general(a, b, (((1,), (0,)), ((), ())), preferred_element_type=F32)


def dot_nt(a, b):
    return lax.dot_general(a, b, (((1,), (1,)), ((), ())), preferred_element_type=F32)


def dot_tn(a, b):
    return lax.dot_general(a, b, (((0,), (0,)), ((), ())), preferred_element_type=F32)


def permutation():
    order = []
    for tile in range(6):
        order += [SLICE * tile + lane for lane in range(96)]
        source = 6 if tile < 3 else 7
        order += [SLICE * source + 32 * (tile % 3) + lane for lane in range(32)]
    return order


def rcopy(src, dst, send, recv, dev):
    return pltpu.make_async_remote_copy(
        src_ref=src, dst_ref=dst, send_sem=send, recv_sem=recv, device_id=dev, device_id_type=MESH
    )


def kernel(
    acts, packed, labels, wf_h, ws_h, wd_h, wa_h, wc_h,
    gf, gs, gd, ga, gc,
    rawx, x, feat, hid, pat, wf, ws, wd, wa, wc,
    pooled, auxall, poolall, stats, logits, backs, backr, agall, pgrad,
    target, acc_f, acc_s, acc_d, gaacc,
    pf, ps, pd, rf, rs, rd,
    local, psend, precv, dsend, drecv,
):
    me_s = lax.axis_index("section")
    me_d = lax.axis_index("dp")

    def act_copy(image):
        return pltpu.make_async_copy(
            acts.at[0, image], rawx.at[image], local.at[image]
        )

    own_copy = pltpu.make_async_copy(packed, pat.at[me_s], local.at[16])
    own_copy.start()
    weights = [
        pltpu.make_async_copy(src.at[0], dst, local.at[17 + i])
        for i, (src, dst) in enumerate(((wf_h, wf), (ws_h, ws), (wa_h, wa), (wc_h, wc)))
    ] + [pltpu.make_async_copy(wd_h, wd, local.at[21])]
    weights[0].start()
    weights[1].start()
    for image in range(IMG):
        act_copy(image).start()
    for copy in weights[2:]:
        copy.start()

    barrier = pltpu.get_barrier_semaphore()

    def greet_s(k, _):
        pl.semaphore_signal(barrier, inc=1, device_id={"section": lax.rem(me_s + k, SEC)}, device_id_type=MESH)
        return 0

    def greet_d(k, _):
        pl.semaphore_signal(barrier, inc=1, device_id={"dp": lax.rem(me_d + k, DP)}, device_id_type=MESH)
        return 0

    lax.fori_loop(1, SEC, greet_s, 0)
    lax.fori_loop(1, DP, greet_d, 0)
    pl.semaphore_wait(barrier, SEC - 1 + DP - 1)

    own_copy.wait()

    def patch_copy(chunk, peer):
        return rcopy(
            pat.at[me_s, chunk], pat.at[me_s, chunk],
            psend.at[chunk, peer], precv.at[chunk, me_s], {"section": peer},
        )

    for chunk in range(CHUNKS):
        def send_patch(k, _, chunk=chunk):
            patch_copy(chunk, lax.rem(me_s + k, SEC)).start()
            return 0

        lax.fori_loop(1, SEC, send_patch, 0)

    weights[0].wait()
    weights[1].wait()

    def forward(chunk, _):
        base = pl.multiple_of(chunk * CROWS, CROWS)

        def wait_act(a, _):
            image = chunk * PER + a
            pltpu.make_async_copy(
                acts.at[0, image], rawx.at[image], local.at[image]
            ).wait()
            start = pl.multiple_of(image * PAD, PAD)
            x[pl.ds(start + 192, 16), :] = jnp.zeros((16, C), BF16)
            x[pl.ds(start, PIX), :] = rawx[image]
            return 0

        lax.fori_loop(0, PER, wait_act, 0)
        xc = x[pl.ds(base, CROWS), :]
        h = jnp.maximum(dot(xc, wf[...]), 0.0).astype(BF16)
        hid[pl.ds(base, CROWS), :] = h
        f = (xc.astype(F32) + dot(h, ws[...])).astype(BF16)
        feat[pl.ds(base, CROWS), :] = f
        for a in range(PER):
            part = f[a * PAD:(a + 1) * PAD, :].astype(F32)
            pooled[pl.ds(chunk * PER + a, 1), :] = jnp.sum(part, axis=0, keepdims=True) * (1.0 / PIX)
        return 0

    lax.fori_loop(0, CHUNKS, forward, 0)

    def spread(kind, src, dst):
        def one(k, _):
            peer = lax.rem(me_d + k, DP)
            rcopy(src(peer), dst, dsend.at[kind, peer], drecv.at[kind, me_d], {"dp": peer}).start()
            return 0

        lax.fori_loop(1, DP, one, 0)

    def collect(kind, slot):
        def one(k, _):
            peer = lax.rem(me_d + k, DP)
            rcopy(slot(peer), slot(peer), dsend.at[kind, peer], drecv.at[kind, peer], {"dp": peer}).wait_recv()
            return 0

        lax.fori_loop(1, DP, one, 0)

    weights[2].wait()
    weights[3].wait()
    weights[4].wait()
    pool_b = pooled[...].astype(BF16)
    aux_out = jnp.maximum(dot(pool_b, wa[...]), 0.0).astype(BF16)
    auxall[me_d] = aux_out
    spread(0, lambda peer: auxall.at[me_d], auxall.at[me_d])
    for block in range(8):
        poolall[DP, block] = pool_b[:, 128 * block:128 * (block + 1)]
    poolall_own = poolall[DP, me_d // 2]
    poolall[me_d, 0] = poolall_own
    spread(1, lambda peer: poolall.at[DP, peer // 2], poolall.at[me_d, 0])

    collect(0, lambda peer: auxall.at[peer])
    every = auxall[...].reshape(DP * IMG, HEAD)
    raw = dot_nt(wc[...], every)
    logits[...] = raw
    top = jnp.max(raw, axis=0, keepdims=True)
    total = jnp.sum(jnp.exp(raw - top), axis=0, keepdims=True)
    lane = lax.broadcasted_iota(jnp.int32, (1, DP * IMG), 1)
    row = jnp.zeros((1, DP * IMG), F32)
    for image in range(IMG):
        row = jnp.where(lane == me_d * IMG + image, labels[image].astype(F32), row)
    stats[me_d] = jnp.concatenate([top, total, row, jnp.zeros((5, DP * IMG), F32)], axis=0)
    spread(2, lambda peer: stats.at[me_d], stats.at[me_d])
    collect(2, lambda peer: stats.at[peer])
    table = stats[...]
    tops, totals, rows = table[:, 0, :], table[:, 1, :], table[:, 2, :]
    high = jnp.max(tops, axis=0, keepdims=True)
    denominator = jnp.sum(totals * jnp.exp(tops - high), axis=0, keepdims=True)
    label = jnp.sum(rows, axis=0, keepdims=True).astype(jnp.int32)
    prob = jnp.exp(logits[...] - high) / denominator
    number = lax.broadcasted_iota(jnp.int32, (CSHARD, DP * IMG), 0) + me_d * CSHARD
    lg = ((prob - (number == label).astype(F32)) * 0.0625).astype(BF16)
    gc[0] = dot(lg, every)
    backs[...] = dot_tn(lg, wc[...]).reshape(DP, IMG, HEAD)
    spread(3, lambda peer: backs.at[peer], backr.at[me_d])
    backr[me_d] = backs[me_d]
    collect(3, lambda peer: backr.at[peer])
    back = jnp.sum(backr[...], axis=0)
    aux_grad = jnp.where(aux_out > 0, back, 0.0).astype(BF16)
    agall[me_d] = aux_grad
    spread(4, lambda peer: agall.at[me_d], agall.at[me_d])
    pgrad[...] = dot_nt(aux_grad, wa[...]) * (1.0 / PIX)
    collect(1, lambda peer: poolall.at[peer, 0])
    collect(4, lambda peer: agall.at[peer])
    gaacc[...] = jnp.zeros_like(gaacc)

    def aux_part(group, _):
        part = dot_tn(poolall[group, 0], agall[group]).astype(BF16)
        gaacc[...] += part.astype(F32)
        return 0

    lax.fori_loop(0, DP, aux_part, 0)
    ga[0] = gaacc[pl.ds(pl.multiple_of(64 * lax.rem(me_d, 2), 64), 64), :]

    lane96 = lax.broadcasted_iota(jnp.int32, (PAD, 128), 1)

    def backward(chunk, _):
        base = pl.multiple_of(chunk * CROWS, CROWS)

        def wait_patch(k, _):
            peer = lax.rem(me_s + k, SEC)
            rcopy(
                pat.at[peer, chunk], pat.at[peer, chunk],
                psend.at[chunk, peer], precv.at[chunk, peer], {"section": peer},
            ).wait_recv()
            return 0

        lax.fori_loop(1, SEC, wait_patch, 0)

        for tile in range(6):
            filler, sub = (6 if tile < 3 else 7), tile % 3
            columns = pl.ds(tile * 128, 128)
            for a in range(3):
                main = pat[tile, chunk, pl.ds(a * PAD, PAD), :].astype(F32)
                extra = pat[filler, chunk, pl.ds(a * PAD, PAD), :].astype(F32)
                if sub < 3:
                    extra = pltpu.roll(extra, 96 - 32 * sub, 1)
                target[pl.ds(a * PAD, PAD), columns] = jnp.where(lane96 < 96, main, extra).astype(BF16)
            p0 = pltpu.roll(pat[tile, chunk, pl.ds(0, PAD), :].astype(F32), 32, 1)
            p1 = pltpu.roll(pat[tile, chunk, pl.ds(PAD, PAD), :].astype(F32), 64, 1)
            p2 = pltpu.roll(pat[tile, chunk, pl.ds(2 * PAD, PAD), :].astype(F32), 96, 1)
            extra = pat[filler, chunk, pl.ds(sub * PAD, PAD), :].astype(F32)
            last = jnp.where(lane96 < 32, p0, jnp.where(lane96 < 64, p1, jnp.where(lane96 < 96, p2, extra)))
            target[pl.ds(3 * PAD, PAD), columns] = last.astype(BF16)

        f = feat[pl.ds(base, CROWS), :]
        recon = dot(f, wd[...])
        rg = ((recon - target[...].astype(F32)) * (1.0 / 224.0)).astype(BF16)
        part = dot_tn(f, rg)

        @pl.when(chunk == 0)
        def _():
            acc_d[...] = part

        @pl.when(chunk > 0)
        def _():
            acc_d[...] += part

        back = dot_nt(rg, wd[...])
        parts = []
        for a in range(PER):
            parts.append(back[a * PAD:(a + 1) * PAD, :] + pgrad[pl.ds(chunk * PER + a, 1), :])
        fg = jnp.concatenate(parts, axis=0).astype(BF16)
        h = hid[pl.ds(base, CROWS), :]
        hg = jnp.where(h > 0, dot_nt(fg, ws[...]), 0.0).astype(BF16)
        part_s = dot_tn(h, fg)
        part_f = dot_tn(x[pl.ds(base, CROWS), :], hg)

        @pl.when(chunk == 0)
        def _():
            acc_s[...] = part_s
            acc_f[...] = part_f

        @pl.when(chunk > 0)
        def _():
            acc_s[...] += part_s
            acc_f[...] += part_f

        return 0

    lax.fori_loop(0, CHUNKS, backward, 0)

    pd[...] = acc_d[...].astype(BF16).reshape(DP, 64, PATCH)
    spread(5, lambda peer: pd.at[peer], rd.at[me_d])
    pf[...] = acc_f[...].astype(BF16).reshape(DP, 64, BOT)
    spread(6, lambda peer: pf.at[peer], rf.at[me_d])
    ps[...] = acc_s[...].astype(BF16).reshape(DP, 16, C)
    spread(7, lambda peer: ps.at[peer], rs.at[me_d])
    rd[me_d] = pd[me_d]
    rf[me_d] = pf[me_d]
    rs[me_d] = ps[me_d]

    def finish(kind, got, out):
        collect(kind, lambda peer: got.at[peer])
        out[0] = got[0].astype(F32)

        def one(group, _):
            out[0] += got[group].astype(F32)
            return 0

        lax.fori_loop(1, DP, one, 0)

    finish(5, rd, gd)
    finish(6, rf, gf)
    finish(7, rs, gs)

    def drain_patch(k, _):
        peer = lax.rem(me_s + k, SEC)
        for chunk in range(CHUNKS):
            patch_copy(chunk, peer).wait_send()
        return 0

    lax.fori_loop(1, SEC, drain_patch, 0)

    def drain(k, _):
        peer = lax.rem(me_d + k, DP)
        for kind, src in (
            (0, auxall.at[me_d]), (1, poolall.at[DP, 0]), (2, stats.at[me_d]), (3, backs.at[peer]),
            (4, agall.at[me_d]), (5, pd.at[peer]), (6, pf.at[peer]), (7, ps.at[peer]),
        ):
            rcopy(src, src, dsend.at[kind, peer], drecv.at[kind, peer], {"dp": peer}).wait_send()
        return 0

    lax.fori_loop(1, DP, drain, 0)


def pack(patches):
    four = jnp.pad(patches, ((0, 0), (0, PAD - PIX), (0, 0))).reshape(CHUNKS, PER, PAD, SLICE)
    main = four[:, :3]
    extra = jnp.transpose(four[:, 3].reshape(CHUNKS, PAD, 3, 32), (0, 2, 1, 3))
    return jnp.concatenate([main, extra], axis=3).reshape(CHUNKS, PROWS, 128)


def local_step(acts, patches, labels, w_first, w_second, w_decode, w_aux, w_class):
    order = permutation()
    pieces, start = [], 0
    for tile in range(6):
        source = 6 if tile < 3 else 7
        pieces.append(w_decode[0][:, SLICE * tile:SLICE * (tile + 1)])
        begin = SLICE * source + 32 * (tile % 3)
        pieces.append(w_decode[0][:, begin:begin + 32])
    decode = jnp.concatenate(pieces, axis=1)
    any_spec = pl.BlockSpec(memory_space=pl.ANY)
    vmem = pl.BlockSpec(memory_space=pltpu.VMEM)
    shapes = [
        ((IMG, PIX, C), BF16), ((IMG * PAD, C), BF16), ((IMG * PAD, C), BF16), ((IMG * PAD, BOT), BF16),
        ((SEC, CHUNKS, PROWS, 128), BF16),
        ((C, BOT), BF16), ((BOT, C), BF16), ((C, PATCH), BF16), ((C, HEAD), BF16), ((CSHARD, HEAD), BF16),
        ((IMG, C), F32), ((DP, IMG, HEAD), BF16), ((DP + 1, 8, IMG, 128), BF16), ((DP, 8, DP * IMG), F32),
        ((CSHARD, DP * IMG), F32), ((DP, IMG, HEAD), F32), ((DP, IMG, HEAD), F32), ((DP, IMG, HEAD), BF16),
        ((IMG, C), F32),
        ((CROWS, PATCH), BF16), ((C, BOT), F32), ((BOT, C), F32), ((C, PATCH), F32), ((128, HEAD), F32),
        ((DP, 64, BOT), BF16), ((DP, 16, C), BF16), ((DP, 64, PATCH), BF16),
        ((DP, 64, BOT), BF16), ((DP, 16, C), BF16), ((DP, 64, PATCH), BF16),
    ]
    gf, gs, gd, ga, gc = pl.pallas_call(
        kernel,
        name="step",
        out_shape=(
            jax.ShapeDtypeStruct((1, 64, BOT), F32), jax.ShapeDtypeStruct((1, 16, C), F32),
            jax.ShapeDtypeStruct((1, 64, PATCH), F32), jax.ShapeDtypeStruct((1, 64, HEAD), F32),
            jax.ShapeDtypeStruct((1, CSHARD, HEAD), F32),
        ),
        in_specs=[any_spec, any_spec, pl.BlockSpec(memory_space=pltpu.SMEM)] + [any_spec] * 5,
        out_specs=[vmem] * 5,
        scratch_shapes=[pltpu.VMEM(shape, kind) for shape, kind in shapes] + [
            pltpu.SemaphoreType.DMA((22,)),
            pltpu.SemaphoreType.DMA((CHUNKS, SEC)), pltpu.SemaphoreType.DMA((CHUNKS, SEC)),
            pltpu.SemaphoreType.DMA((8, DP)), pltpu.SemaphoreType.DMA((8, DP)),
        ],
        compiler_params=pltpu.CompilerParams(
            collective_id=0, has_side_effects=True, vmem_limit_bytes=63 * 2**20
        ),
        cost_estimate=pl.CostEstimate(flops=25 * 10**9, bytes_accessed=16 * 10**6, transcendentals=400000),
    )(acts, pack(patches), labels, w_first, w_second, decode, w_aux, w_class)
    back = [None] * SEC
    for tile in range(6):
        back[tile] = gd[:, :, 128 * tile:128 * tile + SLICE]
    for source in (6, 7):
        tiles = range(3) if source == 6 else range(3, 6)
        back[source] = jnp.concatenate([gd[:, :, 128 * tile + SLICE:128 * (tile + 1)] for tile in tiles], axis=2)
    return gf, gs, jnp.concatenate(back, axis=2), ga, gc


def solution(mesh):
    in_specs = (
        P("section", "dp", None, None),
        P("dp", None, "section"),
        P("dp"),
        P("section", None, None),
        P("section", None, None),
        P("section", None, None),
        P("section", None, None),
        P("section", "dp", None),
    )
    out_specs = (P("section", "dp", None),) * 5
    return jax.shard_map(local_step, mesh=mesh, in_specs=in_specs, out_specs=out_specs, check_vma=False)
```

```python
import jax
import jax.numpy as jnp
from jax import lax
from jax.experimental import pallas as pl
from jax.experimental.pallas import tpu as pltpu
from jax.sharding import PartitionSpec as P

MESH = pl.DeviceIdType.MESH
F32 = jnp.float32
BF16 = jnp.bfloat16

C = 1024
BOT = 256
PIX = 196
PATCH = 768
HEAD = 512
CLASSES = 11264
SEC = 8
DP = 16
IMG = 16
ROWS = PIX * IMG
SLICE = PATCH // SEC
CSHARD = CLASSES // DP
STARTS = (0, 768, 1536, 2304)
SIZES = (768, 768, 768, 832)
CHUNKS = len(SIZES)
PROWS = ROWS * SLICE // 128
KINDS = (2, 1, 2, 1)


def dot(a, b):
    return lax.dot_general(a, b, (((1,), (0,)), ((), ())), preferred_element_type=F32)


def dot_nt(a, b):
    return lax.dot_general(a, b, (((1,), (1,)), ((), ())), preferred_element_type=F32)


def dot_tn(a, b):
    return lax.dot_general(a, b, (((0,), (0,)), ((), ())), preferred_element_type=F32)


def rcopy(src, dst, send, recv, dev):
    return pltpu.make_async_remote_copy(
        src_ref=src, dst_ref=dst, send_sem=send, recv_sem=recv, device_id=dev, device_id_type=MESH
    )


def half_rows(chunk, half):
    start, size = STARTS[chunk] * 3 // 4, SIZES[chunk] * 3 // 4
    first = size // 32 * 16
    return pl.ds(start, first) if half == 0 else pl.ds(start + first, size - first)


def kernel(
    acts, packed, labels, wf_h, ws_h, wd_h, wa_h, wc_h,
    gf, gs, gd, ga, gc,
    x, feat, hid, pat, wf, ws, wd, wp, wa, wc, recon,
    pooled, poolb, auxall, poolall, stats, logits, backs, backr, agall, pgrad,
    target, acc_f, acc_s, acc_d, gaacc,
    pf, ps, pd, qf, qs, qd, tf, ts, td, rf, rs, rd,
    local, psend, precv, dsend, drecv, csend, crecv, tsend, trecv,
):
    me_s = lax.axis_index("section")
    me_d = lax.axis_index("dp")
    side = me_s // 4
    row = lax.rem(me_s, 4)
    core = lax.rem(me_d, 2)
    chip = me_d // 2

    def at(where, step):
        return where * 4 + lax.rem(row + step, 4)

    up, down, across = at(side, 1), at(side, 3), at(1 - side, 0)

    loads = [
        pltpu.make_async_copy(src, dst, local.at[i])
        for i, (src, dst) in enumerate(
            [(packed, pat.at[me_s]), (wf_h.at[0], wf), (ws_h.at[0], ws)]
            + [
                (acts.at[pl.ds(STARTS[c], SIZES[c]), :], x.at[pl.ds(STARTS[c], SIZES[c]), :])
                for c in range(CHUNKS)
            ]
            + [(wa_h.at[0], wa), (wd_h.at[0], wd), (wc_h.at[0], wc)]
        )
    ]
    for load in loads:
        load.start()

    barrier = pltpu.get_barrier_semaphore()
    for peer in (up, down, across):
        pl.semaphore_signal(barrier, inc=1, device_id={"section": peer}, device_id_type=MESH)

    def greet(k, _):
        pl.semaphore_signal(barrier, inc=1, device_id={"dp": lax.rem(me_d + k, DP)}, device_id_type=MESH)
        return 0

    lax.fori_loop(1, DP, greet, 0)
    pl.semaphore_wait(barrier, 3 + DP - 1)

    sent = [0] * CHUNKS
    started = []

    def pass_on(chunk, source, half, peer):
        place = pat.at[source, half_rows(chunk, half), :]
        copy = rcopy(
            place, place, psend.at[chunk, sent[chunk]], precv.at[chunk, half, source], {"section": peer}
        )
        sent[chunk] += 1
        copy.start()
        started.append(copy)

    def arrive(chunk, source, half):
        place = pat.at[source, half_rows(chunk, half), :]
        rcopy(
            place, place, psend.at[chunk, 0], precv.at[chunk, half, source], {"section": up}
        ).wait_recv()

    loads[0].wait()
    for chunk in range(CHUNKS):
        for half in range(2):
            pass_on(chunk, me_s, half, across)
            pass_on(chunk, me_s, half, up if half == 0 else down)
            pass_on(chunk, me_s, half, down if half == 0 else up)

    def stage1(chunk):
        for source, half, onward in (
            (at(side, 3), 0, up), (at(side, 1), 1, down), (at(side, 3), 1, None), (at(side, 1), 0, None)
        ):
            arrive(chunk, source, half)
            if onward is not None:
                pass_on(chunk, source, half, onward)
            if KINDS[chunk] == 1:
                pass_on(chunk, source, half, across)
        if KINDS[chunk] == 2:
            for half in range(2):
                arrive(chunk, across, half)
                pass_on(chunk, across, half, up if half == 0 else down)
                pass_on(chunk, across, half, down if half == 0 else up)

    def stage2(chunk):
        if KINDS[chunk] == 1:
            for half in range(2):
                arrive(chunk, at(side, 2), half)
                pass_on(chunk, at(side, 2), half, across)
        else:
            arrive(chunk, at(1 - side, 3), 0)
            pass_on(chunk, at(1 - side, 3), 0, up)
            arrive(chunk, at(1 - side, 1), 1)
            pass_on(chunk, at(1 - side, 1), 1, down)

    def stage3(chunk):
        if KINDS[chunk] == 1:
            for step in (0, 1, 3, 2):
                for half in range(2):
                    arrive(chunk, at(1 - side, step), half)
        else:
            arrive(chunk, at(1 - side, 3), 1)
            arrive(chunk, at(1 - side, 1), 0)
            for half in range(2):
                arrive(chunk, at(side, 2), half)
                arrive(chunk, at(1 - side, 2), half)

    def rows_of(chunk):
        return pl.ds(STARTS[chunk], SIZES[chunk])

    def forward(chunk):
        loads[3 + chunk].wait()
        xc = x[rows_of(chunk), :]
        h = jnp.maximum(dot(xc, wf[...]), 0.0).astype(BF16)
        hid[rows_of(chunk), :] = h
        f = (xc.astype(F32) + dot(h, ws[...])).astype(BF16)
        feat[rows_of(chunk), :] = f
        part = jnp.sum(f.astype(F32).reshape(SIZES[chunk] // IMG, IMG, C), axis=0)
        if chunk == 0:
            pooled[...] = part
        else:
            pooled[...] += part

    def rebuild(chunk):
        recon[rows_of(chunk), :] = dot(feat[rows_of(chunk), :], wp[...])

    def spread(kind, src, dst):
        def one(k, _):
            peer = lax.rem(me_d + k, DP)
            rcopy(src(peer), dst, dsend.at[kind, peer], drecv.at[kind, me_d], {"dp": peer}).start()
            return 0

        lax.fori_loop(1, DP, one, 0)

    def collect(kind, slot):
        def one(k, _):
            peer = lax.rem(me_d + k, DP)
            rcopy(slot(peer), slot(peer), dsend.at[kind, peer], drecv.at[kind, peer], {"dp": peer}).wait_recv()
            return 0

        lax.fori_loop(1, DP, one, 0)

    loads[1].wait()
    loads[2].wait()
    forward(0)
    forward(1)
    stage1(0)
    forward(2)
    forward(3)

    loads[7].wait()
    pool_b = (pooled[...] * (1.0 / PIX)).astype(BF16)
    aux_out = jnp.maximum(dot(pool_b, wa[...]), 0.0).astype(BF16)
    auxall[me_d] = aux_out
    spread(0, lambda peer: auxall.at[me_d], auxall.at[me_d])
    for block in range(8):
        poolb[block] = pool_b[:, 128 * block:128 * (block + 1)]
    poolall[me_d] = poolb[chip]
    spread(1, lambda peer: poolb.at[peer // 2], poolall.at[me_d])
    stage1(1)

    loads[8].wait()
    source = lax.broadcasted_iota(jnp.int32, (PATCH, PATCH), 0)
    place = lax.broadcasted_iota(jnp.int32, (PATCH, PATCH), 1)
    tile, lane = place >> 7, place & 127
    late = (tile >= 3).astype(jnp.int32)
    origin = jnp.where(
        lane < SLICE, SLICE * tile + lane, 6 * SLICE + SLICE * late + 32 * (tile - 3 * late) + lane - SLICE
    )
    wp[...] = dot(wd[...], (source == origin).astype(F32).astype(BF16)).astype(BF16)
    rebuild(0)

    loads[9].wait()
    collect(0, lambda peer: auxall.at[peer])
    every = auxall[...].reshape(DP * IMG, HEAD)
    raw = dot_nt(wc[...], every)
    logits[...] = raw
    top = jnp.max(raw, axis=0, keepdims=True)
    total = jnp.sum(jnp.exp(raw - top), axis=0, keepdims=True)
    column = lax.broadcasted_iota(jnp.int32, (1, DP * IMG), 1)
    line = jnp.zeros((1, DP * IMG), F32)
    for image in range(IMG):
        line = jnp.where(column == me_d * IMG + image, labels[image].astype(F32), line)
    stats[me_d] = jnp.concatenate([top, total, line, jnp.zeros((5, DP * IMG), F32)], axis=0)
    spread(2, lambda peer: stats.at[me_d], stats.at[me_d])
    stage2(0)
    stage1(2)
    rebuild(1)

    collect(2, lambda peer: stats.at[peer])
    table = stats[...]
    high = jnp.max(table[:, 0, :], axis=0, keepdims=True)
    denominator = jnp.sum(table[:, 1, :] * jnp.exp(table[:, 0, :] - high), axis=0, keepdims=True)
    label = jnp.sum(table[:, 2, :], axis=0, keepdims=True).astype(jnp.int32)
    prob = jnp.exp(logits[...] - high) / denominator
    number = lax.broadcasted_iota(jnp.int32, (CSHARD, DP * IMG), 0) + me_d * CSHARD
    lg = ((prob - (number == label).astype(F32)) * 0.0625).astype(BF16)
    backs[...] = dot_tn(lg, wc[...]).reshape(DP, IMG, HEAD)
    spread(3, lambda peer: backs.at[peer], backr.at[me_d])
    backr[me_d] = backs[me_d]
    gc[0] = dot(lg, every)
    stage2(1)
    stage1(3)
    rebuild(2)

    collect(3, lambda peer: backr.at[peer])
    aux_grad = jnp.where(auxall[me_d] > 0, jnp.sum(backr[...], axis=0), 0.0).astype(BF16)
    agall[me_d] = aux_grad
    spread(4, lambda peer: agall.at[me_d], agall.at[me_d])
    pgrad[...] = dot_nt(aux_grad, wa[...]) * (1.0 / PIX)
    stage2(2)
    stage2(3)
    rebuild(3)

    def assemble(chunk):
        q = SIZES[chunk] // 4
        base = STARTS[chunk] * 3 // 4
        cut = lax.broadcasted_iota(jnp.int32, (q, 128), 1)
        for tile in range(6):
            filler, sub = (6 if tile < 3 else 7), tile % 3
            columns = pl.ds(tile * 128, 128)
            blocks = [pat[tile, pl.ds(base + a * q, q), :].astype(F32) for a in range(3)]
            for a in range(3):
                extra = pltpu.roll(pat[filler, pl.ds(base + a * q, q), :].astype(F32), 96 - 32 * sub, 1)
                target[pl.ds(a * q, q), columns] = jnp.where(cut < 96, blocks[a], extra).astype(BF16)
            turned = [pltpu.roll(blocks[a], 32 * (a + 1), 1) for a in range(3)]
            extra = pat[filler, pl.ds(base + sub * q, q), :].astype(F32)
            last = jnp.where(cut < 64, jnp.where(cut < 32, turned[0], turned[1]), jnp.where(cut < 96, turned[2], extra))
            target[pl.ds(3 * q, q), columns] = last.astype(BF16)

    def decode_grad(chunk):
        stage3(chunk)
        assemble(chunk)
        size = SIZES[chunk]
        rg = ((recon[rows_of(chunk), :] - target[pl.ds(0, size), :].astype(F32)) * (1.0 / 224.0)).astype(BF16)
        part = dot_tn(feat[rows_of(chunk), :], rg)
        if chunk == 0:
            acc_d[...] = part
        else:
            acc_d[...] += part
        return rg

    def feature_grad(chunk, rg):
        size = SIZES[chunk]
        back = dot_nt(rg, wp[...]).reshape(size // IMG, IMG, C) + pgrad[...][None]
        fg = back.reshape(size, C).astype(BF16)
        h = hid[rows_of(chunk), :]
        hg = jnp.where(h > 0, dot_nt(fg, ws[...]), 0.0).astype(BF16)
        return fg, hg

    def module_grads(chunk, fg, hg):
        part_s = dot_tn(hid[rows_of(chunk), :], fg)
        part_f = dot_tn(x[rows_of(chunk), :], hg)
        if chunk == 0:
            acc_s[...] = part_s
            acc_f[...] = part_f
        else:
            acc_s[...] += part_s
            acc_f[...] += part_f

    for chunk in range(CHUNKS - 1):
        rg = decode_grad(chunk)
        module_grads(chunk, *feature_grad(chunk, rg))

    collect(1, lambda peer: poolall.at[peer])
    collect(4, lambda peer: agall.at[peer])
    gaacc[...] = jnp.zeros_like(gaacc)

    def aux_part(group, _):
        gaacc[...] += dot_tn(poolall[group], agall[group]).astype(BF16).astype(F32)
        return 0

    lax.fori_loop(0, DP, aux_part, 0)
    ga[0] = gaacc[pl.ds(pl.multiple_of(64 * core, 64), 64), :]

    def pair(kind, mine, theirs):
        return rcopy(mine.at[1 - core], theirs, csend.at[kind], crecv.at[kind], {"dp": me_d + 1 - 2 * core})

    def split(acc, out, rows):
        whole = acc[...].astype(BF16).reshape(8, 2, rows, acc.shape[1])
        out[0] = whole[:, 0]
        out[1] = whole[:, 1]

    def chip_sum(kind, mine, theirs, out, got):
        pair(kind, mine, theirs).wait_recv()
        out[...] = (mine[core].astype(F32) + theirs[...].astype(F32)).astype(BF16)

        def one(k, _):
            peer = lax.rem(chip + k, 8)
            rcopy(
                out.at[peer], got.at[chip], tsend.at[kind, peer], trecv.at[kind, chip], {"dp": 2 * peer + core}
            ).start()
            return 0

        lax.fori_loop(1, 8, one, 0)
        got[chip] = out[chip]

    def total_sum(kind, got):
        def one(k, _):
            peer = lax.rem(chip + k, 8)
            rcopy(
                got.at[peer], got.at[peer], tsend.at[kind, peer], trecv.at[kind, peer], {"dp": 2 * peer + core}
            ).wait_recv()
            return 0

        lax.fori_loop(1, 8, one, 0)
        return jnp.sum(got[...].astype(F32), axis=0)

    last = CHUNKS - 1
    rg = decode_grad(last)
    split(acc_d, pd, 64)
    pair(0, pd, qd).start()
    fg, hg = feature_grad(last, rg)
    chip_sum(0, pd, qd, td, rd)
    module_grads(last, fg, hg)
    split(acc_f, pf, 64)
    pair(1, pf, qf).start()
    split(acc_s, ps, 16)
    pair(2, ps, qs).start()
    chip_sum(1, pf, qf, tf, rf)
    chip_sum(2, ps, qs, ts, rs)

    gsum = total_sum(0, rd)
    for s in range(SEC):
        if s < 6:
            gd[0, :, SLICE * s:SLICE * (s + 1)] = gsum[:, 128 * s:128 * s + SLICE]
        else:
            for sub in range(3):
                begin = 128 * (3 * (s - 6) + sub) + SLICE
                gd[0, :, SLICE * s + 32 * sub:SLICE * s + 32 * (sub + 1)] = gsum[:, begin:begin + 32]
    gf[0] = total_sum(1, rf)
    gs[0] = total_sum(2, rs)

    for copy in started:
        copy.wait_send()
    for kind, mine, theirs in ((0, pd, qd), (1, pf, qf), (2, ps, qs)):
        pair(kind, mine, theirs).wait_send()

    def drain(k, _):
        peer = lax.rem(me_d + k, DP)
        for kind, src in (
            (0, auxall.at[me_d]), (1, poolb.at[0]), (2, stats.at[me_d]), (3, backs.at[peer]), (4, agall.at[me_d])
        ):
            rcopy(src, src, dsend.at[kind, peer], drecv.at[kind, peer], {"dp": peer}).wait_send()
        return 0

    lax.fori_loop(1, DP, drain, 0)

    def drain_chip(k, _):
        peer = lax.rem(chip + k, 8)
        for kind, src in ((0, td), (1, tf), (2, ts)):
            rcopy(
                src.at[peer], src.at[peer], tsend.at[kind, peer], trecv.at[kind, peer], {"dp": 2 * peer + core}
            ).wait_send()
        return 0

    lax.fori_loop(1, 8, drain_chip, 0)


def pack(patches):
    rows = jnp.transpose(patches, (1, 0, 2)).reshape(ROWS, SLICE)
    parts = []
    for chunk in range(CHUNKS):
        q = SIZES[chunk] // 4
        four = lax.slice_in_dim(rows, STARTS[chunk], STARTS[chunk] + SIZES[chunk]).reshape(4, q, SLICE)
        extra = jnp.transpose(four[3].reshape(q, 3, 32), (1, 0, 2))
        parts.append(jnp.concatenate([four[:3], extra], axis=2).reshape(3 * q, 128))
    return jnp.concatenate(parts, axis=0)


def local_step(acts, patches, labels, w_first, w_second, w_decode, w_aux, w_class):
    any_spec = pl.BlockSpec(memory_space=pl.ANY)
    vmem = pl.BlockSpec(memory_space=pltpu.VMEM)
    big = max(SIZES)
    shapes = [
        ((ROWS, C), BF16), ((ROWS, C), BF16), ((ROWS, BOT), BF16), ((SEC, PROWS, 128), BF16),
        ((C, BOT), BF16), ((BOT, C), BF16), ((C, PATCH), BF16), ((C, PATCH), BF16), ((C, HEAD), BF16),
        ((CSHARD, HEAD), BF16), ((ROWS, PATCH), F32),
        ((IMG, C), F32), ((8, IMG, 128), BF16), ((DP, IMG, HEAD), BF16), ((DP, IMG, 128), BF16),
        ((DP, 8, DP * IMG), F32), ((CSHARD, DP * IMG), F32), ((DP, IMG, HEAD), F32), ((DP, IMG, HEAD), F32),
        ((DP, IMG, HEAD), BF16), ((IMG, C), F32),
        ((big, PATCH), BF16), ((C, BOT), F32), ((BOT, C), F32), ((C, PATCH), F32), ((128, HEAD), F32),
        ((2, 8, 64, BOT), BF16), ((2, 8, 16, C), BF16), ((2, 8, 64, PATCH), BF16),
    ] + [((8, 64, BOT), BF16), ((8, 16, C), BF16), ((8, 64, PATCH), BF16)] * 3
    return pl.pallas_call(
        kernel,
        name="step",
        out_shape=(
            jax.ShapeDtypeStruct((1, 64, BOT), F32), jax.ShapeDtypeStruct((1, 16, C), F32),
            jax.ShapeDtypeStruct((1, 64, PATCH), F32), jax.ShapeDtypeStruct((1, 64, HEAD), F32),
            jax.ShapeDtypeStruct((1, CSHARD, HEAD), F32),
        ),
        in_specs=[any_spec, any_spec, pl.BlockSpec(memory_space=pltpu.SMEM)] + [any_spec] * 5,
        out_specs=[vmem] * 5,
        scratch_shapes=[pltpu.VMEM(shape, kind) for shape, kind in shapes] + [
            pltpu.SemaphoreType.DMA((10,)),
            pltpu.SemaphoreType.DMA((CHUNKS, 14)), pltpu.SemaphoreType.DMA((CHUNKS, 2, SEC)),
            pltpu.SemaphoreType.DMA((5, DP)), pltpu.SemaphoreType.DMA((5, DP)),
            pltpu.SemaphoreType.DMA((3,)), pltpu.SemaphoreType.DMA((3,)),
            pltpu.SemaphoreType.DMA((3, 8)), pltpu.SemaphoreType.DMA((3, 8)),
        ],
        compiler_params=pltpu.CompilerParams(
            collective_id=0, has_side_effects=True, vmem_limit_bytes=63 * 2**20
        ),
        cost_estimate=pl.CostEstimate(flops=25 * 10**9, bytes_accessed=16 * 10**6, transcendentals=400000),
    )(
        jnp.transpose(acts[0], (1, 0, 2)).reshape(ROWS, C), pack(patches), labels,
        w_first, w_second, w_decode, w_aux, w_class,
    )


def solution(mesh):
    in_specs = (
        P("section", "dp", None, None),
        P("dp", None, "section"),
        P("dp"),
        P("section", None, None),
        P("section", None, None),
        P("section", None, None),
        P("section", None, None),
        P("section", "dp", None),
    )
    out_specs = (P("section", "dp", None),) * 5
    return jax.shard_map(local_step, mesh=mesh, in_specs=in_specs, out_specs=out_specs, check_vma=False)
```

```python
import jax
import jax.numpy as jnp
from jax import lax
from jax.experimental import pallas as pl
from jax.experimental.pallas import tpu as pltpu
from jax.sharding import PartitionSpec as P

MESH = pl.DeviceIdType.MESH
F32 = jnp.float32
BF16 = jnp.bfloat16

C = 1024
BOT = 256
PIX = 196
PATCH = 768
HEAD = 512
CLASSES = 11264
SEC = 8
DP = 16
IMG = 16
ROWS = PIX * IMG
SLICE = PATCH // SEC
CSHARD = CLASSES // DP
STARTS = (0, 768, 1536, 2304)
SIZES = (768, 768, 768, 832)
CHUNKS = len(SIZES)
PROWS = ROWS * SLICE // 128
KINDS = (2, 2, 1, 2)


def dot(a, b):
    return lax.dot_general(a, b, (((1,), (0,)), ((), ())), preferred_element_type=F32)


def dot_nt(a, b):
    return lax.dot_general(a, b, (((1,), (1,)), ((), ())), preferred_element_type=F32)


def dot_tn(a, b):
    return lax.dot_general(a, b, (((0,), (0,)), ((), ())), preferred_element_type=F32)


def rcopy(src, dst, send, recv, dev):
    return pltpu.make_async_remote_copy(
        src_ref=src, dst_ref=dst, send_sem=send, recv_sem=recv, device_id=dev, device_id_type=MESH
    )


def half_rows(chunk, half):
    start, size = STARTS[chunk] * 3 // 4, SIZES[chunk] * 3 // 4
    first = size // 32 * 16
    return pl.ds(start, first) if half == 0 else pl.ds(start + first, size - first)


def kernel(
    acts, patches, labels, wf_h, ws_h, wd_h, wa_h, wc_h,
    gf, gs, gd, ga, gc,
    x, feat, hid, pat, raw, wf, ws, wd, wp, wa, wc, recon,
    pooled, poolb, auxall, poolall, stats, logits, backs, backr, agall, pgrad,
    target, acc_f, acc_s, acc_d, gaacc,
    pf, ps, pd, qf, qs, qd, tf, ts, td, rf, rs, rd,
    local, psend, precv, dsend, drecv, csend, crecv, tsend, trecv,
):
    me_s = lax.axis_index("section")
    me_d = lax.axis_index("dp")
    side = me_s // 4
    row = lax.rem(me_s, 4)
    core = lax.rem(me_d, 2)
    chip = me_d // 2

    def at(where, step):
        return where * 4 + lax.rem(row + step, 4)

    up, down, across = at(side, 1), at(side, 3), at(1 - side, 0)

    loads = [
        pltpu.make_async_copy(src, dst, local.at[i])
        for i, (src, dst) in enumerate(
            [(patches, raw), (wf_h.at[0], wf), (ws_h.at[0], ws)]
            + [
                (acts.at[pl.ds(STARTS[c], SIZES[c]), :], x.at[pl.ds(STARTS[c], SIZES[c]), :])
                for c in range(CHUNKS)
            ]
            + [(wa_h.at[0], wa), (wd_h.at[0], wd), (wc_h.at[0], wc)]
        )
    ]
    for load in loads:
        load.start()

    barrier = pltpu.get_barrier_semaphore()
    for peer in (up, down, across):
        pl.semaphore_signal(barrier, inc=1, device_id={"section": peer}, device_id_type=MESH)

    def greet(k, _):
        pl.semaphore_signal(barrier, inc=1, device_id={"dp": lax.rem(me_d + k, DP)}, device_id_type=MESH)
        return 0

    lax.fori_loop(1, DP, greet, 0)

    sent = [0] * CHUNKS
    started = []

    def pass_on(chunk, source, half, peer):
        place = pat.at[source, half_rows(chunk, half), :]
        copy = rcopy(
            place, place, psend.at[chunk, sent[chunk]], precv.at[chunk, half, source], {"section": peer}
        )
        sent[chunk] += 1
        copy.start()
        started.append(copy)

    def arrive(chunk, source, half):
        place = pat.at[source, half_rows(chunk, half), :]
        rcopy(
            place, place, psend.at[chunk, 0], precv.at[chunk, half, source], {"section": up}
        ).wait_recv()

    def own_y(chunk):
        for half in range(2):
            pass_on(chunk, me_s, half, up if half == 0 else down)
            pass_on(chunk, me_s, half, down if half == 0 else up)

    def own_x(chunk):
        for half in range(2):
            pass_on(chunk, me_s, half, across)

    def pack(chunk):
        q = SIZES[chunk] // 4
        base = STARTS[chunk] * 3 // 4
        fourth = raw[pl.ds(STARTS[chunk] + 3 * q, q), :]
        for a in range(3):
            pat[me_s, pl.ds(base + a * q, q), 0:SLICE] = raw[pl.ds(STARTS[chunk] + a * q, q), :]
            pat[me_s, pl.ds(base + a * q, q), SLICE:128] = fourth[:, 32 * a:32 * (a + 1)]

    def stage1(chunk):
        for source, half, onward in (
            (at(side, 3), 0, up), (at(side, 1), 1, down), (at(side, 3), 1, None), (at(side, 1), 0, None)
        ):
            arrive(chunk, source, half)
            if onward is not None:
                pass_on(chunk, source, half, onward)
            if KINDS[chunk] == 1:
                pass_on(chunk, source, half, across)
        if KINDS[chunk] == 2:
            for half in range(2):
                arrive(chunk, across, half)
                pass_on(chunk, across, half, up if half == 0 else down)
                pass_on(chunk, across, half, down if half == 0 else up)

    def stage2(chunk):
        if KINDS[chunk] == 1:
            for half in range(2):
                arrive(chunk, at(side, 2), half)
                pass_on(chunk, at(side, 2), half, across)
        else:
            arrive(chunk, at(1 - side, 3), 0)
            pass_on(chunk, at(1 - side, 3), 0, up)
            arrive(chunk, at(1 - side, 1), 1)
            pass_on(chunk, at(1 - side, 1), 1, down)

    def stage3(chunk):
        if KINDS[chunk] == 1:
            for step in (0, 1, 3, 2):
                for half in range(2):
                    arrive(chunk, at(1 - side, step), half)
        else:
            arrive(chunk, at(1 - side, 3), 1)
            arrive(chunk, at(1 - side, 1), 0)
            for half in range(2):
                arrive(chunk, at(side, 2), half)
                arrive(chunk, at(1 - side, 2), half)

    def rows_of(chunk):
        return pl.ds(STARTS[chunk], SIZES[chunk])

    def forward(chunk):
        loads[3 + chunk].wait()
        xc = x[rows_of(chunk), :]
        h = jnp.maximum(dot(xc, wf[...]), 0.0).astype(BF16)
        hid[rows_of(chunk), :] = h
        f = (xc.astype(F32) + dot(h, ws[...])).astype(BF16)
        feat[rows_of(chunk), :] = f
        part = jnp.sum(f.astype(F32).reshape(SIZES[chunk] // IMG, IMG, C), axis=0)
        if chunk == 0:
            pooled[...] = part
        else:
            pooled[...] += part

    def rebuild(chunk):
        recon[rows_of(chunk), :] = dot(feat[rows_of(chunk), :], wp[...])

    def assemble(chunk):
        q = SIZES[chunk] // 4
        base = STARTS[chunk] * 3 // 4
        cut = lax.broadcasted_iota(jnp.int32, (q, 128), 1)
        for tile in range(6):
            filler, sub = (6 if tile < 3 else 7), tile % 3
            columns = pl.ds(tile * 128, 128)
            blocks = [pat[tile, pl.ds(base + a * q, q), :].astype(F32) for a in range(3)]
            for a in range(3):
                extra = pltpu.roll(pat[filler, pl.ds(base + a * q, q), :].astype(F32), 96 - 32 * sub, 1)
                target[pl.ds(a * q, q), columns] = jnp.where(cut < 96, blocks[a], extra).astype(BF16)
            turned = [pltpu.roll(blocks[a], 32 * (a + 1), 1) for a in range(3)]
            extra = pat[filler, pl.ds(base + sub * q, q), :].astype(F32)
            last = jnp.where(cut < 64, jnp.where(cut < 32, turned[0], turned[1]), jnp.where(cut < 96, turned[2], extra))
            target[pl.ds(3 * q, q), columns] = last.astype(BF16)

    def decode_grad(chunk):
        stage3(chunk)
        assemble(chunk)
        size = SIZES[chunk]
        rg = ((recon[rows_of(chunk), :] - target[pl.ds(0, size), :].astype(F32)) * (1.0 / 224.0)).astype(BF16)
        part = dot_tn(feat[rows_of(chunk), :], rg)
        if chunk == 0:
            acc_d[...] = part
        else:
            acc_d[...] += part
        return rg

    def feature_grad(chunk, rg):
        size = SIZES[chunk]
        back = dot_nt(rg, wp[...]).reshape(size // IMG, IMG, C) + pgrad[...][None]
        fg = back.reshape(size, C).astype(BF16)
        h = hid[rows_of(chunk), :]
        hg = jnp.where(h > 0, dot_nt(fg, ws[...]), 0.0).astype(BF16)
        return fg, hg

    def module_grads(chunk, fg, hg):
        part_s = dot_tn(hid[rows_of(chunk), :], fg)
        part_f = dot_tn(x[rows_of(chunk), :], hg)
        if chunk == 0:
            acc_s[...] = part_s
            acc_f[...] = part_f
        else:
            acc_s[...] += part_s
            acc_f[...] += part_f

    def spread(kind, src, dst):
        def one(k, _):
            peer = lax.rem(me_d + k, DP)
            rcopy(src(peer), dst, dsend.at[kind, peer], drecv.at[kind, me_d], {"dp": peer}).start()
            return 0

        lax.fori_loop(1, DP, one, 0)

    def collect(kind, slot):
        def one(k, _):
            peer = lax.rem(me_d + k, DP)
            rcopy(slot(peer), slot(peer), dsend.at[kind, peer], drecv.at[kind, peer], {"dp": peer}).wait_recv()
            return 0

        lax.fori_loop(1, DP, one, 0)

    loads[0].wait()
    for chunk in range(CHUNKS):
        pack(chunk)
    loads[1].wait()
    loads[2].wait()
    forward(0)
    pl.semaphore_wait(barrier, 3 + DP - 1)
    own_x(0)
    own_y(0)
    own_y(1)
    forward(1)
    forward(2)
    forward(3)

    loads[7].wait()
    pool_b = (pooled[...] * (1.0 / PIX)).astype(BF16)
    aux_out = jnp.maximum(dot(pool_b, wa[...]), 0.0).astype(BF16)
    auxall[me_d] = aux_out
    spread(0, lambda peer: auxall.at[me_d], auxall.at[me_d])
    for block in range(8):
        poolb[block] = pool_b[:, 128 * block:128 * (block + 1)]
    poolall[me_d] = poolb[chip]
    own_x(1)

    loads[8].wait()
    source = lax.broadcasted_iota(jnp.int32, (PATCH, PATCH), 0)
    place = lax.broadcasted_iota(jnp.int32, (PATCH, PATCH), 1)
    tile, lane = place >> 7, place & 127
    late = (tile >= 3).astype(jnp.int32)
    origin = jnp.where(
        lane < SLICE, SLICE * tile + lane, 6 * SLICE + SLICE * late + 32 * (tile - 3 * late) + lane - SLICE
    )
    wp[...] = dot(wd[...], (source == origin).astype(F32).astype(BF16)).astype(BF16)
    stage1(0)
    own_y(2)
    rebuild(0)
    rebuild(1)
    rebuild(2)

    loads[9].wait()
    collect(0, lambda peer: auxall.at[peer])
    every = auxall[...].reshape(DP * IMG, HEAD)
    score = dot_nt(wc[...], every)
    logits[...] = score
    top = jnp.max(score, axis=0, keepdims=True)
    total = jnp.sum(jnp.exp(score - top), axis=0, keepdims=True)
    column = lax.broadcasted_iota(jnp.int32, (1, DP * IMG), 1)
    line = jnp.zeros((1, DP * IMG), F32)
    for image in range(IMG):
        line = jnp.where(column == me_d * IMG + image, labels[image].astype(F32), line)
    stats[me_d] = jnp.concatenate([top, total, line, jnp.zeros((5, DP * IMG), F32)], axis=0)
    spread(2, lambda peer: stats.at[me_d], stats.at[me_d])
    own_x(3)
    rebuild(3)
    stage1(1)

    collect(2, lambda peer: stats.at[peer])
    table = stats[...]
    high = jnp.max(table[:, 0, :], axis=0, keepdims=True)
    denominator = jnp.sum(table[:, 1, :] * jnp.exp(table[:, 0, :] - high), axis=0, keepdims=True)
    label = jnp.sum(table[:, 2, :], axis=0, keepdims=True).astype(jnp.int32)
    prob = jnp.exp(logits[...] - high) / denominator
    number = lax.broadcasted_iota(jnp.int32, (CSHARD, DP * IMG), 0) + me_d * CSHARD
    lg = ((prob - (number == label).astype(F32)) * 0.0625).astype(BF16)
    backs[...] = dot_tn(lg, wc[...]).astype(BF16).reshape(DP, IMG, HEAD)
    spread(3, lambda peer: backs.at[peer], backr.at[me_d])
    backr[me_d] = backs[me_d]
    gc[0] = dot(lg, every)
    stage2(0)
    own_x(2)
    stage1(2)
    rg = decode_grad(0)

    collect(3, lambda peer: backr.at[peer])
    aux_grad = jnp.where(auxall[me_d] > 0, jnp.sum(backr[...].astype(F32), axis=0), 0.0).astype(BF16)
    agall[me_d] = aux_grad
    spread(4, lambda peer: agall.at[me_d], agall.at[me_d])
    spread(1, lambda peer: poolb.at[peer // 2], poolall.at[me_d])
    pgrad[...] = dot_nt(aux_grad, wa[...]) * (1.0 / PIX)
    stage2(1)
    own_y(3)
    module_grads(0, *feature_grad(0, rg))
    stage2(2)
    rg = decode_grad(1)
    stage1(3)
    module_grads(1, *feature_grad(1, rg))
    collect(1, lambda peer: poolall.at[peer])
    collect(4, lambda peer: agall.at[peer])
    sums = jnp.zeros((128, HEAD), F32)
    for group in range(DP):
        sums += dot_tn(poolall[group], agall[group]).astype(BF16).astype(F32)
    gaacc[...] = sums
    ga[0] = gaacc[pl.ds(pl.multiple_of(64 * core, 64), 64), :]
    rg = decode_grad(2)
    stage2(3)
    module_grads(2, *feature_grad(2, rg))

    def pair(kind, mine, theirs):
        return rcopy(mine.at[1 - core], theirs, csend.at[kind], crecv.at[kind], {"dp": me_d + 1 - 2 * core})

    def split(acc, out, rows):
        whole = acc[...].astype(BF16).reshape(8, 2, rows, acc.shape[1])
        out[0] = whole[:, 0]
        out[1] = whole[:, 1]

    def chip_sum(kind, mine, theirs, out, got):
        pair(kind, mine, theirs).wait_recv()
        out[...] = (mine[core].astype(F32) + theirs[...].astype(F32)).astype(BF16)

        def one(k, _):
            peer = lax.rem(chip + k, 8)
            rcopy(
                out.at[peer], got.at[chip], tsend.at[kind, peer], trecv.at[kind, chip], {"dp": 2 * peer + core}
            ).start()
            return 0

        lax.fori_loop(1, 8, one, 0)
        got[chip] = out[chip]

    def total_sum(kind, got):
        def one(k, _):
            peer = lax.rem(chip + k, 8)
            rcopy(
                got.at[peer], got.at[peer], tsend.at[kind, peer], trecv.at[kind, peer], {"dp": 2 * peer + core}
            ).wait_recv()
            return 0

        lax.fori_loop(1, 8, one, 0)
        return jnp.sum(got[...].astype(F32), axis=0)

    last = CHUNKS - 1
    rg = decode_grad(last)
    split(acc_d, pd, 64)
    pair(0, pd, qd).start()
    fg, hg = feature_grad(last, rg)
    chip_sum(0, pd, qd, td, rd)
    module_grads(last, fg, hg)
    split(acc_f, pf, 64)
    pair(1, pf, qf).start()
    split(acc_s, ps, 16)
    pair(2, ps, qs).start()
    chip_sum(1, pf, qf, tf, rf)
    chip_sum(2, ps, qs, ts, rs)

    gsum = total_sum(0, rd)
    for s in range(SEC):
        if s < 6:
            gd[0, :, SLICE * s:SLICE * (s + 1)] = gsum[:, 128 * s:128 * s + SLICE]
        else:
            for sub in range(3):
                begin = 128 * (3 * (s - 6) + sub) + SLICE
                gd[0, :, SLICE * s + 32 * sub:SLICE * s + 32 * (sub + 1)] = gsum[:, begin:begin + 32]
    gf[0] = total_sum(1, rf)
    gs[0] = total_sum(2, rs)

    for copy in started:
        copy.wait_send()
    for kind, mine, theirs in ((0, pd, qd), (1, pf, qf), (2, ps, qs)):
        pair(kind, mine, theirs).wait_send()

    def drain(k, _):
        peer = lax.rem(me_d + k, DP)
        for kind, src in (
            (0, auxall.at[me_d]), (1, poolb.at[0]), (2, stats.at[me_d]), (3, backs.at[peer]), (4, agall.at[me_d])
        ):
            rcopy(src, src, dsend.at[kind, peer], drecv.at[kind, peer], {"dp": peer}).wait_send()
        return 0

    lax.fori_loop(1, DP, drain, 0)

    def drain_chip(k, _):
        peer = lax.rem(chip + k, 8)
        for kind, src in ((0, td), (1, tf), (2, ts)):
            rcopy(
                src.at[peer], src.at[peer], tsend.at[kind, peer], trecv.at[kind, peer], {"dp": 2 * peer + core}
            ).wait_send()
        return 0

    lax.fori_loop(1, 8, drain_chip, 0)


def finish(*refs):
    sems = refs[-1]
    copies = [pltpu.make_async_copy(refs[i], refs[5 + i], sems.at[i]) for i in range(5)]
    for copy in copies:
        copy.start()
    for copy in copies:
        copy.wait()


def local_step(acts, patches, labels, w_first, w_second, w_decode, w_aux, w_class):
    any_spec = pl.BlockSpec(memory_space=pl.ANY)
    vmem = pl.BlockSpec(memory_space=pltpu.VMEM)
    big = max(SIZES)
    shapes = [
        ((ROWS, C), BF16), ((ROWS, C), BF16), ((ROWS, BOT), BF16), ((SEC, PROWS, 128), BF16), ((ROWS, SLICE), BF16),
        ((C, BOT), BF16), ((BOT, C), BF16), ((C, PATCH), BF16), ((C, PATCH), BF16), ((C, HEAD), BF16),
        ((CSHARD, HEAD), BF16), ((ROWS, PATCH), F32),
        ((IMG, C), F32), ((8, IMG, 128), BF16), ((DP, IMG, HEAD), BF16), ((DP, IMG, 128), BF16),
        ((DP, 8, DP * IMG), F32), ((CSHARD, DP * IMG), F32), ((DP, IMG, HEAD), BF16), ((DP, IMG, HEAD), BF16),
        ((DP, IMG, HEAD), BF16), ((IMG, C), F32),
        ((big, PATCH), BF16), ((C, BOT), F32), ((BOT, C), F32), ((C, PATCH), F32), ((128, HEAD), F32),
        ((2, 8, 64, BOT), BF16), ((2, 8, 16, C), BF16), ((2, 8, 64, PATCH), BF16),
    ] + [((8, 64, BOT), BF16), ((8, 16, C), BF16), ((8, 64, PATCH), BF16)] * 3
    shapes_out = (
        jax.ShapeDtypeStruct((1, 64, BOT), F32), jax.ShapeDtypeStruct((1, 16, C), F32),
        jax.ShapeDtypeStruct((1, 64, PATCH), F32), jax.ShapeDtypeStruct((1, 64, HEAD), F32),
        jax.ShapeDtypeStruct((1, CSHARD, HEAD), F32),
    )
    results = pl.pallas_call(
        kernel,
        name="step",
        out_shape=shapes_out,
        in_specs=[any_spec, any_spec, pl.BlockSpec(memory_space=pltpu.SMEM)] + [any_spec] * 5,
        out_specs=[vmem] * 5,
        scratch_shapes=[pltpu.VMEM(shape, kind) for shape, kind in shapes] + [
            pltpu.SemaphoreType.DMA((10,)),
            pltpu.SemaphoreType.DMA((CHUNKS, 14)), pltpu.SemaphoreType.DMA((CHUNKS, 2, SEC)),
            pltpu.SemaphoreType.DMA((5, DP)), pltpu.SemaphoreType.DMA((5, DP)),
            pltpu.SemaphoreType.DMA((3,)), pltpu.SemaphoreType.DMA((3,)),
            pltpu.SemaphoreType.DMA((3, 8)), pltpu.SemaphoreType.DMA((3, 8)),
        ],
        compiler_params=pltpu.CompilerParams(
            collective_id=0, has_side_effects=True, vmem_limit_bytes=63 * 2**20
        ),
        cost_estimate=pl.CostEstimate(flops=25 * 10**9, bytes_accessed=16 * 10**6, transcendentals=400000),
    )(
        jnp.transpose(acts[0], (1, 0, 2)).reshape(ROWS, C),
        jnp.transpose(patches, (1, 0, 2)).reshape(ROWS, SLICE), labels,
        w_first, w_second, w_decode, w_aux, w_class,
    )
    return pl.pallas_call(
        finish,
        name="finish",
        out_shape=shapes_out,
        in_specs=[any_spec] * 5,
        out_specs=[any_spec] * 5,
        scratch_shapes=[pltpu.SemaphoreType.DMA((5,))],
    )(*results)


def solution(mesh):
    in_specs = (
        P("section", "dp", None, None),
        P("dp", None, "section"),
        P("dp"),
        P("section", None, None),
        P("section", None, None),
        P("section", None, None),
        P("section", None, None),
        P("section", "dp", None),
    )
    out_specs = (P("section", "dp", None),) * 5
    return jax.shard_map(local_step, mesh=mesh, in_specs=in_specs, out_specs=out_specs, check_vma=False)
```

```python
import jax
import jax.numpy as jnp
from jax import lax
from jax.experimental import pallas as pl
from jax.experimental.pallas import tpu as pltpu
from jax.sharding import PartitionSpec as P

MESH = pl.DeviceIdType.MESH
F32 = jnp.float32
BF16 = jnp.bfloat16

C = 1024
BOT = 256
PIX = 196
PATCH = 768
HEAD = 512
CLASSES = 11264
SEC = 8
DP = 16
IMG = 16
ROWS = PIX * IMG
SLICE = PATCH // SEC
CSHARD = CLASSES // DP
STARTS = (0, 768, 1536, 2304)
SIZES = (768, 768, 768, 832)
CHUNKS = len(SIZES)
PROWS = ROWS * SLICE // 128
KINDS = (2, 2, 1, 2)


def dot(a, b):
    return lax.dot_general(a, b, (((1,), (0,)), ((), ())), preferred_element_type=F32)


def dot_nt(a, b):
    return lax.dot_general(a, b, (((1,), (1,)), ((), ())), preferred_element_type=F32)


def dot_tn(a, b):
    return lax.dot_general(a, b, (((0,), (0,)), ((), ())), preferred_element_type=F32)


def rcopy(src, dst, send, recv, dev):
    return pltpu.make_async_remote_copy(
        src_ref=src, dst_ref=dst, send_sem=send, recv_sem=recv, device_id=dev, device_id_type=MESH
    )


def half_rows(chunk, half):
    start, size = STARTS[chunk] * 3 // 4, SIZES[chunk] * 3 // 4
    first = size // 32 * 16
    return pl.ds(start, first) if half == 0 else pl.ds(start + first, size - first)


def kernel(
    acts, patches, labels, wf_h, ws_h, wd_h, wa_h, wc_h,
    gf, gs, gd, ga, gc,
    x, feat, hid, pat, raw, wf, ws, wd, wp, wa, wc, recon,
    pooled, poolb, auxall, poolall, stats, logits, backs, backr, agall, pgrad,
    target, acc_f, acc_s, acc_d, gaacc,
    pf, ps, pd, qf, qs, qd, tf, ts, td, rf, rs, rd,
    local, psend, precv, dsend, drecv, csend, crecv, tsend, trecv,
):
    me_s = lax.axis_index("section")
    me_d = lax.axis_index("dp")
    side = me_s // 4
    row = lax.rem(me_s, 4)
    core = lax.rem(me_d, 2)
    chip = me_d // 2

    def at(where, step):
        return where * 4 + lax.rem(row + step, 4)

    up, down, across = at(side, 1), at(side, 3), at(1 - side, 0)

    loads = [
        pltpu.make_async_copy(src, dst, local.at[i])
        for i, (src, dst) in enumerate(
            [(patches, raw), (wf_h.at[0], wf), (ws_h.at[0], ws)]
            + [
                (acts.at[pl.ds(STARTS[c], SIZES[c]), :], x.at[pl.ds(STARTS[c], SIZES[c]), :])
                for c in range(CHUNKS)
            ]
            + [(wa_h.at[0], wa), (wd_h.at[0], wd), (wc_h.at[0], wc)]
        )
    ]
    for load in loads:
        load.start()

    barrier = pltpu.get_barrier_semaphore()
    for peer in (up, down, across):
        pl.semaphore_signal(barrier, inc=1, device_id={"section": peer}, device_id_type=MESH)

    def greet(k, _):
        pl.semaphore_signal(barrier, inc=1, device_id={"dp": lax.rem(me_d + k, DP)}, device_id_type=MESH)
        return 0

    lax.fori_loop(1, DP, greet, 0)

    sent = [0] * CHUNKS
    started = []

    def pass_on(chunk, source, half, peer):
        place = pat.at[source, half_rows(chunk, half), :]
        copy = rcopy(
            place, place, psend.at[chunk, sent[chunk]], precv.at[chunk, half, source], {"section": peer}
        )
        sent[chunk] += 1
        copy.start()
        started.append(copy)

    def arrive(chunk, source, half):
        place = pat.at[source, half_rows(chunk, half), :]
        rcopy(
            place, place, psend.at[chunk, 0], precv.at[chunk, half, source], {"section": up}
        ).wait_recv()

    def own_y(chunk):
        for half in range(2):
            pass_on(chunk, me_s, half, up if half == 0 else down)
            pass_on(chunk, me_s, half, down if half == 0 else up)

    def own_x(chunk):
        for half in range(2):
            pass_on(chunk, me_s, half, across)

    def pack(chunk):
        q = SIZES[chunk] // 4
        base = STARTS[chunk] * 3 // 4
        fourth = raw[pl.ds(STARTS[chunk] + 3 * q, q), :]
        for a in range(3):
            pat[me_s, pl.ds(base + a * q, q), 0:SLICE] = raw[pl.ds(STARTS[chunk] + a * q, q), :]
            pat[me_s, pl.ds(base + a * q, q), SLICE:128] = fourth[:, 32 * a:32 * (a + 1)]

    def stage1(chunk):
        for source, half, onward in (
            (at(side, 3), 0, up), (at(side, 1), 1, down), (at(side, 3), 1, None), (at(side, 1), 0, None)
        ):
            arrive(chunk, source, half)
            if onward is not None:
                pass_on(chunk, source, half, onward)
            if KINDS[chunk] == 1:
                pass_on(chunk, source, half, across)
        if KINDS[chunk] == 2:
            for half in range(2):
                arrive(chunk, across, half)
                pass_on(chunk, across, half, up if half == 0 else down)
                pass_on(chunk, across, half, down if half == 0 else up)

    def stage2(chunk):
        if KINDS[chunk] == 1:
            for half in range(2):
                arrive(chunk, at(side, 2), half)
                pass_on(chunk, at(side, 2), half, across)
        else:
            arrive(chunk, at(1 - side, 3), 0)
            pass_on(chunk, at(1 - side, 3), 0, up)
            arrive(chunk, at(1 - side, 1), 1)
            pass_on(chunk, at(1 - side, 1), 1, down)

    def stage3(chunk):
        if KINDS[chunk] == 1:
            for step in (0, 1, 3, 2):
                for half in range(2):
                    arrive(chunk, at(1 - side, step), half)
        else:
            arrive(chunk, at(1 - side, 3), 1)
            arrive(chunk, at(1 - side, 1), 0)
            for half in range(2):
                arrive(chunk, at(side, 2), half)
                arrive(chunk, at(1 - side, 2), half)

    def rows_of(chunk):
        return pl.ds(STARTS[chunk], SIZES[chunk])

    def forward(chunk):
        loads[3 + chunk].wait()
        xc = x[rows_of(chunk), :]
        h = jnp.maximum(dot(xc, wf[...]), 0.0).astype(BF16)
        hid[rows_of(chunk), :] = h
        f = (xc.astype(F32) + dot(h, ws[...])).astype(BF16)
        feat[rows_of(chunk), :] = f
        part = jnp.sum(f.astype(F32).reshape(SIZES[chunk] // IMG, IMG, C), axis=0)
        if chunk == 0:
            pooled[...] = part
        else:
            pooled[...] += part

    def rebuild(chunk):
        recon[rows_of(chunk), :] = dot(feat[rows_of(chunk), :], wp[...])

    def assemble(chunk):
        q = SIZES[chunk] // 4
        base = STARTS[chunk] * 3 // 4
        cut = lax.broadcasted_iota(jnp.int32, (q, 128), 1)
        for tile in range(6):
            filler, sub = (6 if tile < 3 else 7), tile % 3
            columns = pl.ds(tile * 128, 128)
            blocks = [pat[tile, pl.ds(base + a * q, q), :].astype(F32) for a in range(3)]
            for a in range(3):
                extra = pltpu.roll(pat[filler, pl.ds(base + a * q, q), :].astype(F32), 96 - 32 * sub, 1)
                target[pl.ds(a * q, q), columns] = jnp.where(cut < 96, blocks[a], extra).astype(BF16)
            turned = [pltpu.roll(blocks[a], 32 * (a + 1), 1) for a in range(3)]
            extra = pat[filler, pl.ds(base + sub * q, q), :].astype(F32)
            last = jnp.where(cut < 64, jnp.where(cut < 32, turned[0], turned[1]), jnp.where(cut < 96, turned[2], extra))
            target[pl.ds(3 * q, q), columns] = last.astype(BF16)

    def decode_grad(chunk):
        stage3(chunk)
        assemble(chunk)
        size = SIZES[chunk]
        rg = ((recon[rows_of(chunk), :] - target[pl.ds(0, size), :].astype(F32)) * (1.0 / 224.0)).astype(BF16)
        part = dot_tn(feat[rows_of(chunk), :], rg)
        if chunk == 0:
            acc_d[...] = part
        else:
            acc_d[...] += part
        return rg

    def feature_grad(chunk, rg):
        size = SIZES[chunk]
        back = dot_nt(rg, wp[...]).reshape(size // IMG, IMG, C) + pgrad[...][None]
        fg = back.reshape(size, C).astype(BF16)
        h = hid[rows_of(chunk), :]
        hg = jnp.where(h > 0, dot_nt(fg, ws[...]), 0.0).astype(BF16)
        return fg, hg

    def module_grads(chunk, fg, hg):
        part_s = dot_tn(hid[rows_of(chunk), :], fg)
        part_f = dot_tn(x[rows_of(chunk), :], hg)
        if chunk == 0:
            acc_s[...] = part_s
            acc_f[...] = part_f
        else:
            acc_s[...] += part_s
            acc_f[...] += part_f

    def spread(kind, src, dst):
        def one(k, _):
            peer = lax.rem(me_d + k, DP)
            rcopy(src(peer), dst, dsend.at[kind, peer], drecv.at[kind, me_d], {"dp": peer}).start()
            return 0

        lax.fori_loop(1, DP, one, 0)

    def collect(kind, slot):
        def one(k, _):
            peer = lax.rem(me_d + k, DP)
            rcopy(slot(peer), slot(peer), dsend.at[kind, peer], drecv.at[kind, peer], {"dp": peer}).wait_recv()
            return 0

        lax.fori_loop(1, DP, one, 0)

    loads[0].wait()
    for chunk in range(CHUNKS):
        pack(chunk)
    loads[1].wait()
    loads[2].wait()
    forward(0)
    pl.semaphore_wait(barrier, 3 + DP - 1)
    own_x(0)
    own_y(0)
    own_y(1)
    forward(1)
    forward(2)
    forward(3)

    loads[7].wait()
    pool_b = (pooled[...] * (1.0 / PIX)).astype(BF16)
    aux_out = jnp.maximum(dot(pool_b, wa[...]), 0.0).astype(BF16)
    auxall[me_d] = aux_out
    spread(0, lambda peer: auxall.at[me_d], auxall.at[me_d])
    for block in range(8):
        poolb[block] = pool_b[:, 128 * block:128 * (block + 1)]
    poolall[me_d] = poolb[chip]
    own_x(1)

    loads[8].wait()
    source = lax.broadcasted_iota(jnp.int32, (PATCH, PATCH), 0)
    place = lax.broadcasted_iota(jnp.int32, (PATCH, PATCH), 1)
    tile, lane = place >> 7, place & 127
    late = (tile >= 3).astype(jnp.int32)
    origin = jnp.where(
        lane < SLICE, SLICE * tile + lane, 6 * SLICE + SLICE * late + 32 * (tile - 3 * late) + lane - SLICE
    )
    wp[...] = dot(wd[...], (source == origin).astype(F32).astype(BF16)).astype(BF16)
    stage1(0)
    own_y(2)
    rebuild(0)
    rebuild(1)
    rebuild(2)

    loads[9].wait()
    collect(0, lambda peer: auxall.at[peer])
    every = auxall[...].reshape(DP * IMG, HEAD)
    score = dot_nt(wc[...], every)
    logits[...] = score
    top = jnp.max(score, axis=0, keepdims=True)
    total = jnp.sum(jnp.exp(score - top), axis=0, keepdims=True)
    column = lax.broadcasted_iota(jnp.int32, (1, DP * IMG), 1)
    line = jnp.zeros((1, DP * IMG), F32)
    for image in range(IMG):
        line = jnp.where(column == me_d * IMG + image, labels[image].astype(F32), line)
    stats[me_d] = jnp.concatenate([top, total, line, jnp.zeros((5, DP * IMG), F32)], axis=0)
    spread(2, lambda peer: stats.at[me_d], stats.at[me_d])
    own_x(3)
    rebuild(3)
    stage1(1)

    collect(2, lambda peer: stats.at[peer])
    table = stats[...]
    high = jnp.max(table[:, 0, :], axis=0, keepdims=True)
    denominator = jnp.sum(table[:, 1, :] * jnp.exp(table[:, 0, :] - high), axis=0, keepdims=True)
    label = jnp.sum(table[:, 2, :], axis=0, keepdims=True).astype(jnp.int32)
    prob = jnp.exp(logits[...] - high) / denominator
    number = lax.broadcasted_iota(jnp.int32, (CSHARD, DP * IMG), 0) + me_d * CSHARD
    lg = ((prob - (number == label).astype(F32)) * 0.0625).astype(BF16)
    backs[...] = dot_tn(lg, wc[...]).astype(BF16).reshape(DP, IMG, HEAD)
    spread(3, lambda peer: backs.at[peer], backr.at[me_d])
    backr[me_d] = backs[me_d]
    gc[0] = dot(lg, every)
    stage2(0)
    own_x(2)
    stage1(2)
    rg = decode_grad(0)

    collect(3, lambda peer: backr.at[peer])
    aux_grad = jnp.where(auxall[me_d] > 0, jnp.sum(backr[...].astype(F32), axis=0), 0.0).astype(BF16)
    agall[me_d] = aux_grad
    spread(4, lambda peer: agall.at[me_d], agall.at[me_d])
    spread(1, lambda peer: poolb.at[peer // 2], poolall.at[me_d])
    pgrad[...] = dot_nt(aux_grad, wa[...]) * (1.0 / PIX)
    stage2(1)
    own_y(3)
    module_grads(0, *feature_grad(0, rg))
    stage2(2)
    rg = decode_grad(1)
    stage1(3)
    module_grads(1, *feature_grad(1, rg))
    collect(1, lambda peer: poolall.at[peer])
    collect(4, lambda peer: agall.at[peer])
    sums = jnp.zeros((128, HEAD), F32)
    for group in range(DP):
        sums += dot_tn(poolall[group], agall[group]).astype(BF16).astype(F32)
    gaacc[...] = sums
    ga[0] = gaacc[pl.ds(pl.multiple_of(64 * core, 64), 64), :]
    rg = decode_grad(2)
    stage2(3)
    module_grads(2, *feature_grad(2, rg))

    def pair(kind, mine, theirs):
        return rcopy(mine.at[1 - core], theirs, csend.at[kind], crecv.at[kind], {"dp": me_d + 1 - 2 * core})

    def split(acc, out, rows):
        whole = acc[...].astype(BF16).reshape(8, 2, rows, acc.shape[1])
        out[0] = whole[:, 0]
        out[1] = whole[:, 1]

    def chip_sum(kind, mine, theirs, out, got):
        pair(kind, mine, theirs).wait_recv()
        out[...] = (mine[core].astype(F32) + theirs[...].astype(F32)).astype(BF16)

        def one(k, _):
            peer = lax.rem(chip + k, 8)
            rcopy(
                out.at[peer], got.at[chip], tsend.at[kind, peer], trecv.at[kind, chip], {"dp": 2 * peer + core}
            ).start()
            return 0

        lax.fori_loop(1, 8, one, 0)
        got[chip] = out[chip]

    def total_sum(kind, got):
        def one(k, _):
            peer = lax.rem(chip + k, 8)
            rcopy(
                got.at[peer], got.at[peer], tsend.at[kind, peer], trecv.at[kind, peer], {"dp": 2 * peer + core}
            ).wait_recv()
            return 0

        lax.fori_loop(1, 8, one, 0)
        return jnp.sum(got[...].astype(F32), axis=0)

    last = CHUNKS - 1
    rg = decode_grad(last)
    split(acc_d, pd, 64)
    pair(0, pd, qd).start()
    fg, hg = feature_grad(last, rg)
    chip_sum(0, pd, qd, td, rd)
    module_grads(last, fg, hg)
    split(acc_f, pf, 64)
    pair(1, pf, qf).start()
    split(acc_s, ps, 16)
    pair(2, ps, qs).start()
    chip_sum(1, pf, qf, tf, rf)
    chip_sum(2, ps, qs, ts, rs)

    gsum = total_sum(0, rd)
    for s in range(SEC):
        if s < 6:
            gd[0, :, SLICE * s:SLICE * (s + 1)] = gsum[:, 128 * s:128 * s + SLICE]
        else:
            for sub in range(3):
                begin = 128 * (3 * (s - 6) + sub) + SLICE
                gd[0, :, SLICE * s + 32 * sub:SLICE * s + 32 * (sub + 1)] = gsum[:, begin:begin + 32]
    gf[0] = total_sum(1, rf)
    gs[0] = total_sum(2, rs)

    for copy in started:
        copy.wait_send()
    for kind, mine, theirs in ((0, pd, qd), (1, pf, qf), (2, ps, qs)):
        pair(kind, mine, theirs).wait_send()

    def drain(k, _):
        peer = lax.rem(me_d + k, DP)
        for kind, src in (
            (0, auxall.at[me_d]), (1, poolb.at[0]), (2, stats.at[me_d]), (3, backs.at[peer]), (4, agall.at[me_d])
        ):
            rcopy(src, src, dsend.at[kind, peer], drecv.at[kind, peer], {"dp": peer}).wait_send()
        return 0

    lax.fori_loop(1, DP, drain, 0)

    def drain_chip(k, _):
        peer = lax.rem(chip + k, 8)
        for kind, src in ((0, td), (1, tf), (2, ts)):
            rcopy(
                src.at[peer], src.at[peer], tsend.at[kind, peer], trecv.at[kind, peer], {"dp": 2 * peer + core}
            ).wait_send()
        return 0

    lax.fori_loop(1, 8, drain_chip, 0)


def finish(*refs):
    for source, out in zip(refs[:5], refs[5:]):
        out[...] = source[...]


def local_step(acts, patches, labels, w_first, w_second, w_decode, w_aux, w_class):
    any_spec = pl.BlockSpec(memory_space=pl.ANY)
    vmem = pl.BlockSpec(memory_space=pltpu.VMEM)
    big = max(SIZES)
    shapes = [
        ((ROWS, C), BF16), ((ROWS, C), BF16), ((ROWS, BOT), BF16), ((SEC, PROWS, 128), BF16), ((ROWS, SLICE), BF16),
        ((C, BOT), BF16), ((BOT, C), BF16), ((C, PATCH), BF16), ((C, PATCH), BF16), ((C, HEAD), BF16),
        ((CSHARD, HEAD), BF16), ((ROWS, PATCH), F32),
        ((IMG, C), F32), ((8, IMG, 128), BF16), ((DP, IMG, HEAD), BF16), ((DP, IMG, 128), BF16),
        ((DP, 8, DP * IMG), F32), ((CSHARD, DP * IMG), F32), ((DP, IMG, HEAD), BF16), ((DP, IMG, HEAD), BF16),
        ((DP, IMG, HEAD), BF16), ((IMG, C), F32),
        ((big, PATCH), BF16), ((C, BOT), F32), ((BOT, C), F32), ((C, PATCH), F32), ((128, HEAD), F32),
        ((2, 8, 64, BOT), BF16), ((2, 8, 16, C), BF16), ((2, 8, 64, PATCH), BF16),
    ] + [((8, 64, BOT), BF16), ((8, 16, C), BF16), ((8, 64, PATCH), BF16)] * 3
    shapes_out = (
        jax.ShapeDtypeStruct((1, 64, BOT), F32), jax.ShapeDtypeStruct((1, 16, C), F32),
        jax.ShapeDtypeStruct((1, 64, PATCH), F32), jax.ShapeDtypeStruct((1, 64, HEAD), F32),
        jax.ShapeDtypeStruct((1, CSHARD, HEAD), F32),
    )
    results = pl.pallas_call(
        kernel,
        name="step",
        out_shape=shapes_out,
        in_specs=[any_spec, any_spec, pl.BlockSpec(memory_space=pltpu.SMEM)] + [any_spec] * 5,
        out_specs=[vmem] * 5,
        scratch_shapes=[pltpu.VMEM(shape, kind) for shape, kind in shapes] + [
            pltpu.SemaphoreType.DMA((10,)),
            pltpu.SemaphoreType.DMA((CHUNKS, 14)), pltpu.SemaphoreType.DMA((CHUNKS, 2, SEC)),
            pltpu.SemaphoreType.DMA((5, DP)), pltpu.SemaphoreType.DMA((5, DP)),
            pltpu.SemaphoreType.DMA((3,)), pltpu.SemaphoreType.DMA((3,)),
            pltpu.SemaphoreType.DMA((3, 8)), pltpu.SemaphoreType.DMA((3, 8)),
        ],
        compiler_params=pltpu.CompilerParams(
            collective_id=0, has_side_effects=True, vmem_limit_bytes=63 * 2**20
        ),
        cost_estimate=pl.CostEstimate(flops=25 * 10**9, bytes_accessed=16 * 10**6, transcendentals=400000),
    )(
        jnp.transpose(acts[0], (1, 0, 2)).reshape(ROWS, C),
        jnp.transpose(patches, (1, 0, 2)).reshape(ROWS, SLICE), labels,
        w_first, w_second, w_decode, w_aux, w_class,
    )
    return pl.pallas_call(
        finish,
        name="finish",
        out_shape=shapes_out,
        in_specs=[vmem] * 5,
        out_specs=[vmem] * 5,
    )(*results)


def solution(mesh):
    in_specs = (
        P("section", "dp", None, None),
        P("dp", None, "section"),
        P("dp"),
        P("section", None, None),
        P("section", None, None),
        P("section", None, None),
        P("section", None, None),
        P("section", "dp", None),
    )
    out_specs = (P("section", "dp", None),) * 5
    return jax.shard_map(local_step, mesh=mesh, in_specs=in_specs, out_specs=out_specs, check_vma=False)
```

```python
import jax
import jax.numpy as jnp
from jax import lax
from jax.experimental import pallas as pl
from jax.experimental.pallas import tpu as pltpu
from jax.sharding import PartitionSpec as P

MESH = pl.DeviceIdType.MESH
F32 = jnp.float32
BF16 = jnp.bfloat16

C = 1024
BOT = 256
PIX = 196
PATCH = 768
HEAD = 512
CLASSES = 11264
SEC = 8
DP = 16
IMG = 16
ROWS = PIX * IMG
SLICE = PATCH // SEC
CSHARD = CLASSES // DP
STARTS = (0, 768, 1536, 2304)
SIZES = (768, 768, 768, 832)
CHUNKS = len(SIZES)
PROWS = ROWS * SLICE // 128
KINDS = (2, 2, 1, 2)


def dot(a, b):
    return lax.dot_general(a, b, (((1,), (0,)), ((), ())), preferred_element_type=F32)


def dot_nt(a, b):
    return lax.dot_general(a, b, (((1,), (1,)), ((), ())), preferred_element_type=F32)


def dot_tn(a, b):
    return lax.dot_general(a, b, (((0,), (0,)), ((), ())), preferred_element_type=F32)


def rcopy(src, dst, send, recv, dev):
    return pltpu.make_async_remote_copy(
        src_ref=src, dst_ref=dst, send_sem=send, recv_sem=recv, device_id=dev, device_id_type=MESH
    )


def half_rows(chunk, half):
    start, size = STARTS[chunk] * 3 // 4, SIZES[chunk] * 3 // 4
    first = size // 32 * 16
    return pl.ds(start, first) if half == 0 else pl.ds(start + first, size - first)


def kernel(
    acts, patches, labels, wf_h, ws_h, wd_h, wa_h, wc_h,
    gf, gs, gd, ga, lgs, auxout,
    x, feat, hid, pat, raw, wf, ws, wd, wp, wa, wc, recon,
    pooled, poolb, auxall, poolall, stats, logits, backs, backr, agall, pgrad,
    target, acc_f, acc_s, acc_d, gaacc,
    pf, ps, pd, qf, qs, qd, tf, ts, td, rf, rs, rd,
    local, psend, precv, dsend, drecv, csend, crecv, tsend, trecv,
):
    me_s = lax.axis_index("section")
    me_d = lax.axis_index("dp")
    side = me_s // 4
    row = lax.rem(me_s, 4)
    core = lax.rem(me_d, 2)
    chip = me_d // 2

    def at(where, step):
        return where * 4 + lax.rem(row + step, 4)

    up, down, across = at(side, 1), at(side, 3), at(1 - side, 0)

    loads = [
        pltpu.make_async_copy(src, dst, local.at[i])
        for i, (src, dst) in enumerate(
            [(patches, raw), (wf_h.at[0], wf), (ws_h.at[0], ws)]
            + [
                (acts.at[pl.ds(STARTS[c], SIZES[c]), :], x.at[pl.ds(STARTS[c], SIZES[c]), :])
                for c in range(CHUNKS)
            ]
            + [(wa_h.at[0], wa), (wd_h.at[0], wd), (wc_h.at[0], wc)]
        )
    ]
    for load in loads:
        load.start()

    barrier = pltpu.get_barrier_semaphore()
    for peer in (up, down, across):
        pl.semaphore_signal(barrier, inc=1, device_id={"section": peer}, device_id_type=MESH)

    def greet(k, _):
        pl.semaphore_signal(barrier, inc=1, device_id={"dp": lax.rem(me_d + k, DP)}, device_id_type=MESH)
        return 0

    lax.fori_loop(1, DP, greet, 0)

    sent = [0] * CHUNKS
    started = []

    def pass_on(chunk, source, half, peer):
        place = pat.at[source, half_rows(chunk, half), :]
        copy = rcopy(
            place, place, psend.at[chunk, sent[chunk]], precv.at[chunk, half, source], {"section": peer}
        )
        sent[chunk] += 1
        copy.start()
        started.append(copy)

    def arrive(chunk, source, half):
        place = pat.at[source, half_rows(chunk, half), :]
        rcopy(
            place, place, psend.at[chunk, 0], precv.at[chunk, half, source], {"section": up}
        ).wait_recv()

    def own_y(chunk):
        for half in range(2):
            pass_on(chunk, me_s, half, up if half == 0 else down)
            pass_on(chunk, me_s, half, down if half == 0 else up)

    def own_x(chunk):
        for half in range(2):
            pass_on(chunk, me_s, half, across)

    def pack(chunk):
        q = SIZES[chunk] // 4
        base = STARTS[chunk] * 3 // 4
        fourth = raw[pl.ds(STARTS[chunk] + 3 * q, q), :]
        for a in range(3):
            pat[me_s, pl.ds(base + a * q, q), 0:SLICE] = raw[pl.ds(STARTS[chunk] + a * q, q), :]
            pat[me_s, pl.ds(base + a * q, q), SLICE:128] = fourth[:, 32 * a:32 * (a + 1)]

    def stage1(chunk):
        for source, half, onward in (
            (at(side, 3), 0, up), (at(side, 1), 1, down), (at(side, 3), 1, None), (at(side, 1), 0, None)
        ):
            arrive(chunk, source, half)
            if onward is not None:
                pass_on(chunk, source, half, onward)
            if KINDS[chunk] == 1:
                pass_on(chunk, source, half, across)
        if KINDS[chunk] == 2:
            for half in range(2):
                arrive(chunk, across, half)
                pass_on(chunk, across, half, up if half == 0 else down)
                pass_on(chunk, across, half, down if half == 0 else up)

    def stage2(chunk):
        if KINDS[chunk] == 1:
            for half in range(2):
                arrive(chunk, at(side, 2), half)
                pass_on(chunk, at(side, 2), half, across)
        else:
            arrive(chunk, at(1 - side, 3), 0)
            pass_on(chunk, at(1 - side, 3), 0, up)
            arrive(chunk, at(1 - side, 1), 1)
            pass_on(chunk, at(1 - side, 1), 1, down)

    def stage3(chunk):
        if KINDS[chunk] == 1:
            for step in (0, 1, 3, 2):
                for half in range(2):
                    arrive(chunk, at(1 - side, step), half)
        else:
            arrive(chunk, at(1 - side, 3), 1)
            arrive(chunk, at(1 - side, 1), 0)
            for half in range(2):
                arrive(chunk, at(side, 2), half)
                arrive(chunk, at(1 - side, 2), half)

    def rows_of(chunk):
        return pl.ds(STARTS[chunk], SIZES[chunk])

    def forward(chunk):
        loads[3 + chunk].wait()
        xc = x[rows_of(chunk), :]
        h = jnp.maximum(dot(xc, wf[...]), 0.0).astype(BF16)
        hid[rows_of(chunk), :] = h
        f = (xc.astype(F32) + dot(h, ws[...])).astype(BF16)
        feat[rows_of(chunk), :] = f
        part = jnp.sum(f.astype(F32).reshape(SIZES[chunk] // IMG, IMG, C), axis=0)
        if chunk == 0:
            pooled[...] = part
        else:
            pooled[...] += part

    def rebuild(chunk):
        recon[rows_of(chunk), :] = dot(feat[rows_of(chunk), :], wp[...])

    def assemble(chunk):
        q = SIZES[chunk] // 4
        base = STARTS[chunk] * 3 // 4
        cut = lax.broadcasted_iota(jnp.int32, (q, 128), 1)
        for tile in range(6):
            filler, sub = (6 if tile < 3 else 7), tile % 3
            columns = pl.ds(tile * 128, 128)
            blocks = [pat[tile, pl.ds(base + a * q, q), :].astype(F32) for a in range(3)]
            for a in range(3):
                extra = pltpu.roll(pat[filler, pl.ds(base + a * q, q), :].astype(F32), 96 - 32 * sub, 1)
                target[pl.ds(a * q, q), columns] = jnp.where(cut < 96, blocks[a], extra).astype(BF16)
            turned = [pltpu.roll(blocks[a], 32 * (a + 1), 1) for a in range(3)]
            extra = pat[filler, pl.ds(base + sub * q, q), :].astype(F32)
            last = jnp.where(cut < 64, jnp.where(cut < 32, turned[0], turned[1]), jnp.where(cut < 96, turned[2], extra))
            target[pl.ds(3 * q, q), columns] = last.astype(BF16)

    def decode_grad(chunk):
        stage3(chunk)
        assemble(chunk)
        size = SIZES[chunk]
        rg = ((recon[rows_of(chunk), :] - target[pl.ds(0, size), :].astype(F32)) * (1.0 / 224.0)).astype(BF16)
        part = dot_tn(feat[rows_of(chunk), :], rg)
        if chunk == 0:
            acc_d[...] = part
        else:
            acc_d[...] += part
        return rg

    def feature_grad(chunk, rg):
        size = SIZES[chunk]
        back = dot_nt(rg, wp[...]).reshape(size // IMG, IMG, C) + pgrad[...][None]
        fg = back.reshape(size, C).astype(BF16)
        h = hid[rows_of(chunk), :]
        hg = jnp.where(h > 0, dot_nt(fg, ws[...]), 0.0).astype(BF16)
        return fg, hg

    def module_grads(chunk, fg, hg):
        part_s = dot_tn(hid[rows_of(chunk), :], fg)
        part_f = dot_tn(x[rows_of(chunk), :], hg)
        if chunk == 0:
            acc_s[...] = part_s
            acc_f[...] = part_f
        else:
            acc_s[...] += part_s
            acc_f[...] += part_f

    def spread(kind, src, dst):
        def one(k, _):
            peer = lax.rem(me_d + k, DP)
            rcopy(src(peer), dst, dsend.at[kind, peer], drecv.at[kind, me_d], {"dp": peer}).start()
            return 0

        lax.fori_loop(1, DP, one, 0)

    def collect(kind, slot):
        def one(k, _):
            peer = lax.rem(me_d + k, DP)
            rcopy(slot(peer), slot(peer), dsend.at[kind, peer], drecv.at[kind, peer], {"dp": peer}).wait_recv()
            return 0

        lax.fori_loop(1, DP, one, 0)

    loads[0].wait()
    for chunk in range(CHUNKS):
        pack(chunk)
    loads[1].wait()
    loads[2].wait()
    forward(0)
    pl.semaphore_wait(barrier, 3 + DP - 1)
    own_x(0)
    own_y(0)
    own_y(1)
    forward(1)
    forward(2)
    forward(3)

    loads[7].wait()
    pool_b = (pooled[...] * (1.0 / PIX)).astype(BF16)
    aux_out = jnp.maximum(dot(pool_b, wa[...]), 0.0).astype(BF16)
    auxall[me_d] = aux_out
    spread(0, lambda peer: auxall.at[me_d], auxall.at[me_d])
    for block in range(8):
        poolb[block] = pool_b[:, 128 * block:128 * (block + 1)]
    poolall[me_d] = poolb[chip]
    own_x(1)

    loads[8].wait()
    source = lax.broadcasted_iota(jnp.int32, (PATCH, PATCH), 0)
    place = lax.broadcasted_iota(jnp.int32, (PATCH, PATCH), 1)
    tile, lane = place >> 7, place & 127
    late = (tile >= 3).astype(jnp.int32)
    origin = jnp.where(
        lane < SLICE, SLICE * tile + lane, 6 * SLICE + SLICE * late + 32 * (tile - 3 * late) + lane - SLICE
    )
    wp[...] = dot(wd[...], (source == origin).astype(F32).astype(BF16)).astype(BF16)
    stage1(0)
    own_y(2)
    rebuild(0)
    rebuild(1)

    loads[9].wait()
    collect(0, lambda peer: auxall.at[peer])
    every = auxall[...].reshape(DP * IMG, HEAD)
    score = dot_nt(wc[...], every)
    logits[...] = score
    top = jnp.max(score, axis=0, keepdims=True)
    total = jnp.sum(jnp.exp(score - top), axis=0, keepdims=True)
    column = lax.broadcasted_iota(jnp.int32, (1, DP * IMG), 1)
    line = jnp.zeros((1, DP * IMG), F32)
    for image in range(IMG):
        line = jnp.where(column == me_d * IMG + image, labels[image].astype(F32), line)
    stats[me_d] = jnp.concatenate([top, total, line, jnp.zeros((5, DP * IMG), F32)], axis=0)
    spread(2, lambda peer: stats.at[me_d], stats.at[me_d])
    own_x(3)
    rebuild(2)
    rebuild(3)
    stage2(0)
    stage1(1)

    collect(2, lambda peer: stats.at[peer])
    table = stats[...]
    high = jnp.max(table[:, 0, :], axis=0, keepdims=True)
    denominator = jnp.sum(table[:, 1, :] * jnp.exp(table[:, 0, :] - high), axis=0, keepdims=True)
    label = jnp.sum(table[:, 2, :], axis=0, keepdims=True).astype(jnp.int32)
    prob = jnp.exp(logits[...] - high) / denominator
    number = lax.broadcasted_iota(jnp.int32, (CSHARD, DP * IMG), 0) + me_d * CSHARD
    lg = ((prob - (number == label).astype(F32)) * 0.0625).astype(BF16)
    backs[...] = dot_tn(lg, wc[...]).astype(BF16).reshape(DP, IMG, HEAD)
    spread(3, lambda peer: backs.at[peer], backr.at[me_d])
    backr[me_d] = backs[me_d]
    lgs[...] = lg
    auxout[...] = every
    own_x(2)
    stage1(2)
    own_y(3)
    rg = decode_grad(0)

    collect(3, lambda peer: backr.at[peer])
    aux_grad = jnp.where(auxall[me_d] > 0, jnp.sum(backr[...].astype(F32), axis=0), 0.0).astype(BF16)
    agall[me_d] = aux_grad
    pgrad[...] = dot_nt(aux_grad, wa[...]) * (1.0 / PIX)
    module_grads(0, *feature_grad(0, rg))
    stage2(1)
    stage2(2)
    spread(4, lambda peer: agall.at[me_d], agall.at[me_d])
    spread(1, lambda peer: poolb.at[peer // 2], poolall.at[me_d])
    stage1(3)
    rg = decode_grad(1)
    module_grads(1, *feature_grad(1, rg))
    stage2(3)
    rg_before = decode_grad(2)

    def pair(kind, mine, theirs):
        return rcopy(mine.at[1 - core], theirs, csend.at[kind], crecv.at[kind], {"dp": me_d + 1 - 2 * core})

    def split(acc, out, rows):
        whole = acc[...].astype(BF16).reshape(8, 2, rows, acc.shape[1])
        out[0] = whole[:, 0]
        out[1] = whole[:, 1]

    def chip_sum(kind, mine, theirs, out, got):
        pair(kind, mine, theirs).wait_recv()
        out[...] = (mine[core].astype(F32) + theirs[...].astype(F32)).astype(BF16)

        def one(k, _):
            peer = lax.rem(chip + k, 8)
            rcopy(
                out.at[peer], got.at[chip], tsend.at[kind, peer], trecv.at[kind, chip], {"dp": 2 * peer + core}
            ).start()
            return 0

        lax.fori_loop(1, 8, one, 0)
        got[chip] = out[chip]

    def total_sum(kind, got):
        def one(k, _):
            peer = lax.rem(chip + k, 8)
            rcopy(
                got.at[peer], got.at[peer], tsend.at[kind, peer], trecv.at[kind, peer], {"dp": 2 * peer + core}
            ).wait_recv()
            return 0

        lax.fori_loop(1, 8, one, 0)
        return jnp.sum(got[...].astype(F32), axis=0)

    last = CHUNKS - 1
    rg = decode_grad(last)
    split(acc_d, pd, 64)
    pair(0, pd, qd).start()
    module_grads(last - 1, *feature_grad(last - 1, rg_before))
    chip_sum(0, pd, qd, td, rd)
    module_grads(last, *feature_grad(last, rg))
    split(acc_f, pf, 64)
    pair(1, pf, qf).start()
    split(acc_s, ps, 16)
    pair(2, ps, qs).start()
    chip_sum(1, pf, qf, tf, rf)
    chip_sum(2, ps, qs, ts, rs)

    collect(1, lambda peer: poolall.at[peer])
    collect(4, lambda peer: agall.at[peer])
    sums = jnp.zeros((128, HEAD), F32)
    for group in range(DP):
        sums += dot_tn(poolall[group], agall[group]).astype(BF16).astype(F32)
    gaacc[...] = sums
    ga[0] = gaacc[pl.ds(pl.multiple_of(64 * core, 64), 64), :]
    gsum = total_sum(0, rd)
    for s in range(SEC):
        if s < 6:
            gd[0, :, SLICE * s:SLICE * (s + 1)] = gsum[:, 128 * s:128 * s + SLICE]
        else:
            for sub in range(3):
                begin = 128 * (3 * (s - 6) + sub) + SLICE
                gd[0, :, SLICE * s + 32 * sub:SLICE * s + 32 * (sub + 1)] = gsum[:, begin:begin + 32]
    gf[0] = total_sum(1, rf)
    gs[0] = total_sum(2, rs)

    for copy in started:
        copy.wait_send()
    for kind, mine, theirs in ((0, pd, qd), (1, pf, qf), (2, ps, qs)):
        pair(kind, mine, theirs).wait_send()

    def drain(k, _):
        peer = lax.rem(me_d + k, DP)
        for kind, src in (
            (0, auxall.at[me_d]), (1, poolb.at[0]), (2, stats.at[me_d]), (3, backs.at[peer]), (4, agall.at[me_d])
        ):
            rcopy(src, src, dsend.at[kind, peer], drecv.at[kind, peer], {"dp": peer}).wait_send()
        return 0

    lax.fori_loop(1, DP, drain, 0)

    def drain_chip(k, _):
        peer = lax.rem(chip + k, 8)
        for kind, src in ((0, td), (1, tf), (2, ts)):
            rcopy(
                src.at[peer], src.at[peer], tsend.at[kind, peer], trecv.at[kind, peer], {"dp": 2 * peer + core}
            ).wait_send()
        return 0

    lax.fori_loop(1, 8, drain_chip, 0)


def finish(gf, gs, gd, ga, lgs, auxout, of, os, od, oa, oc):
    for source, out in ((gf, of), (gs, os), (gd, od), (ga, oa)):
        out[...] = source[...]
    oc[0] = dot(lgs[...], auxout[...])


def local_step(acts, patches, labels, w_first, w_second, w_decode, w_aux, w_class):
    any_spec = pl.BlockSpec(memory_space=pl.ANY)
    vmem = pl.BlockSpec(memory_space=pltpu.VMEM)
    big = max(SIZES)
    shapes = [
        ((ROWS, C), BF16), ((ROWS, C), BF16), ((ROWS, BOT), BF16), ((SEC, PROWS, 128), BF16), ((ROWS, SLICE), BF16),
        ((C, BOT), BF16), ((BOT, C), BF16), ((C, PATCH), BF16), ((C, PATCH), BF16), ((C, HEAD), BF16),
        ((CSHARD, HEAD), BF16), ((ROWS, PATCH), F32),
        ((IMG, C), F32), ((8, IMG, 128), BF16), ((DP, IMG, HEAD), BF16), ((DP, IMG, 128), BF16),
        ((DP, 8, DP * IMG), F32), ((CSHARD, DP * IMG), F32), ((DP, IMG, HEAD), BF16), ((DP, IMG, HEAD), BF16),
        ((DP, IMG, HEAD), BF16), ((IMG, C), F32),
        ((big, PATCH), BF16), ((C, BOT), F32), ((BOT, C), F32), ((C, PATCH), F32), ((128, HEAD), F32),
        ((2, 8, 64, BOT), BF16), ((2, 8, 16, C), BF16), ((2, 8, 64, PATCH), BF16),
    ] + [((8, 64, BOT), BF16), ((8, 16, C), BF16), ((8, 64, PATCH), BF16)] * 3
    shapes_out = (
        jax.ShapeDtypeStruct((1, 64, BOT), F32), jax.ShapeDtypeStruct((1, 16, C), F32),
        jax.ShapeDtypeStruct((1, 64, PATCH), F32), jax.ShapeDtypeStruct((1, 64, HEAD), F32),
        jax.ShapeDtypeStruct((1, CSHARD, HEAD), F32),
    )
    results = pl.pallas_call(
        kernel,
        name="step",
        out_shape=shapes_out[:4] + (
            jax.ShapeDtypeStruct((CSHARD, DP * IMG), BF16), jax.ShapeDtypeStruct((DP * IMG, HEAD), BF16),
        ),
        in_specs=[any_spec, any_spec, pl.BlockSpec(memory_space=pltpu.SMEM)] + [any_spec] * 5,
        out_specs=[vmem] * 6,
        scratch_shapes=[pltpu.VMEM(shape, kind) for shape, kind in shapes] + [
            pltpu.SemaphoreType.DMA((10,)),
            pltpu.SemaphoreType.DMA((CHUNKS, 14)), pltpu.SemaphoreType.DMA((CHUNKS, 2, SEC)),
            pltpu.SemaphoreType.DMA((5, DP)), pltpu.SemaphoreType.DMA((5, DP)),
            pltpu.SemaphoreType.DMA((3,)), pltpu.SemaphoreType.DMA((3,)),
            pltpu.SemaphoreType.DMA((3, 8)), pltpu.SemaphoreType.DMA((3, 8)),
        ],
        compiler_params=pltpu.CompilerParams(
            collective_id=0, has_side_effects=True, vmem_limit_bytes=63 * 2**20
        ),
        cost_estimate=pl.CostEstimate(flops=25 * 10**9, bytes_accessed=16 * 10**6, transcendentals=400000),
    )(
        jnp.transpose(acts[0], (1, 0, 2)).reshape(ROWS, C),
        jnp.transpose(patches, (1, 0, 2)).reshape(ROWS, SLICE), labels,
        w_first, w_second, w_decode, w_aux, w_class,
    )
    return pl.pallas_call(
        finish,
        name="finish",
        out_shape=shapes_out,
        in_specs=[vmem] * 6,
        out_specs=[vmem] * 5,
    )(*results)


def solution(mesh):
    in_specs = (
        P("section", "dp", None, None),
        P("dp", None, "section"),
        P("dp"),
        P("section", None, None),
        P("section", None, None),
        P("section", None, None),
        P("section", None, None),
        P("section", "dp", None),
    )
    out_specs = (P("section", "dp", None),) * 5
    return jax.shard_map(local_step, mesh=mesh, in_specs=in_specs, out_specs=out_specs, check_vma=False)
```

```python
import jax
import jax.numpy as jnp
from jax import lax
from jax.experimental import pallas as pl
from jax.experimental.pallas import tpu as pltpu
from jax.sharding import PartitionSpec as P

MESH = pl.DeviceIdType.MESH
F32 = jnp.float32
BF16 = jnp.bfloat16

C = 1024
BOT = 256
PIX = 196
PATCH = 768
HEAD = 512
CLASSES = 11264
SEC = 8
DP = 16
IMG = 16
ROWS = PIX * IMG
SLICE = PATCH // SEC
CSHARD = CLASSES // DP
STARTS = (0, 768, 1536, 2304)
SIZES = (768, 768, 768, 832)
CHUNKS = len(SIZES)
PROWS = ROWS * SLICE // 128
KINDS = (2, 2, 1, 2)


def dot(a, b):
    return lax.dot_general(a, b, (((1,), (0,)), ((), ())), preferred_element_type=F32)


def dot_nt(a, b):
    return lax.dot_general(a, b, (((1,), (1,)), ((), ())), preferred_element_type=F32)


def dot_tn(a, b):
    return lax.dot_general(a, b, (((0,), (0,)), ((), ())), preferred_element_type=F32)


def rcopy(src, dst, send, recv, dev):
    return pltpu.make_async_remote_copy(
        src_ref=src, dst_ref=dst, send_sem=send, recv_sem=recv, device_id=dev, device_id_type=MESH
    )


def half_rows(chunk, half):
    start, size = STARTS[chunk] * 3 // 4, SIZES[chunk] * 3 // 4
    first = size // 32 * 16
    return pl.ds(start, first) if half == 0 else pl.ds(start + first, size - first)


def kernel(
    acts, patches, labels, wf_h, ws_h, wd_h, wa_h, wc_h,
    gf, gs, gd, ga, lgs, auxout,
    x, feat, hid, pat, raw, wf, ws, wd, wp, wa, wc, recon,
    pooled, poolb, auxall, poolall, stats, logits, backs, backr, agall, pgrad,
    target, acc_f, acc_s, acc_d, gaacc,
    pf, ps, pd, qf, qs, qd, tf, ts, td, rf, rs, rd,
    local, psend, precv, dsend, drecv, csend, crecv, tsend, trecv,
):
    me_s = lax.axis_index("section")
    me_d = lax.axis_index("dp")
    side = me_s // 4
    row = lax.rem(me_s, 4)
    core = lax.rem(me_d, 2)
    chip = me_d // 2

    def at(where, step):
        return where * 4 + lax.rem(row + step, 4)

    up, down, across = at(side, 1), at(side, 3), at(1 - side, 0)

    loads = [
        pltpu.make_async_copy(src, dst, local.at[i])
        for i, (src, dst) in enumerate(
            [(patches, raw), (wf_h.at[0], wf), (ws_h.at[0], ws)]
            + [
                (acts.at[pl.ds(STARTS[c], SIZES[c]), :], x.at[pl.ds(STARTS[c], SIZES[c]), :])
                for c in range(CHUNKS)
            ]
            + [(wa_h.at[0], wa), (wd_h.at[0], wd), (wc_h.at[0], wc)]
        )
    ]
    for load in loads:
        load.start()

    barrier = pltpu.get_barrier_semaphore()
    for peer in (up, down, across):
        pl.semaphore_signal(barrier, inc=1, device_id={"section": peer}, device_id_type=MESH)

    def greet(k, _):
        pl.semaphore_signal(barrier, inc=1, device_id={"dp": lax.rem(me_d + k, DP)}, device_id_type=MESH)
        return 0

    lax.fori_loop(1, DP, greet, 0)

    sent = [0] * CHUNKS
    started = []

    def pass_on(chunk, source, half, peer):
        place = pat.at[source, half_rows(chunk, half), :]
        copy = rcopy(
            place, place, psend.at[chunk, sent[chunk]], precv.at[chunk, half, source], {"section": peer}
        )
        sent[chunk] += 1
        copy.start()
        started.append(copy)

    def arrive(chunk, source, half):
        place = pat.at[source, half_rows(chunk, half), :]
        rcopy(
            place, place, psend.at[chunk, 0], precv.at[chunk, half, source], {"section": up}
        ).wait_recv()

    def own_y(chunk):
        for half in range(2):
            pass_on(chunk, me_s, half, up if half == 0 else down)
            pass_on(chunk, me_s, half, down if half == 0 else up)

    def own_x(chunk):
        for half in range(2):
            pass_on(chunk, me_s, half, across)

    def pack(chunk):
        q = SIZES[chunk] // 4
        base = STARTS[chunk] * 3 // 4
        fourth = raw[pl.ds(STARTS[chunk] + 3 * q, q), :]
        for a in range(3):
            pat[me_s, pl.ds(base + a * q, q), 0:SLICE] = raw[pl.ds(STARTS[chunk] + a * q, q), :]
            pat[me_s, pl.ds(base + a * q, q), SLICE:128] = fourth[:, 32 * a:32 * (a + 1)]

    def stage1_across(chunk):
        for half in range(2):
            arrive(chunk, across, half)
            pass_on(chunk, across, half, up if half == 0 else down)
        for half in range(2):
            pass_on(chunk, across, half, down if half == 0 else up)

    def stage1_along(chunk):
        for source, half, onward in (
            (at(side, 3), 0, up), (at(side, 1), 1, down), (at(side, 3), 1, None), (at(side, 1), 0, None)
        ):
            arrive(chunk, source, half)
            if onward is not None:
                pass_on(chunk, source, half, onward)
            if KINDS[chunk] == 1:
                pass_on(chunk, source, half, across)

    def stage1(chunk):
        if KINDS[chunk] == 2:
            stage1_across(chunk)
        stage1_along(chunk)

    def stage2(chunk):
        if KINDS[chunk] == 1:
            for half in range(2):
                arrive(chunk, at(side, 2), half)
                pass_on(chunk, at(side, 2), half, across)
        else:
            arrive(chunk, at(1 - side, 3), 0)
            pass_on(chunk, at(1 - side, 3), 0, up)
            arrive(chunk, at(1 - side, 1), 1)
            pass_on(chunk, at(1 - side, 1), 1, down)

    def stage3(chunk):
        if KINDS[chunk] == 1:
            for step in (0, 1, 3, 2):
                for half in range(2):
                    arrive(chunk, at(1 - side, step), half)
        else:
            arrive(chunk, at(1 - side, 3), 1)
            arrive(chunk, at(1 - side, 1), 0)
            for half in range(2):
                arrive(chunk, at(side, 2), half)
                arrive(chunk, at(1 - side, 2), half)

    def rows_of(chunk):
        return pl.ds(STARTS[chunk], SIZES[chunk])

    def forward(chunk):
        loads[3 + chunk].wait()
        xc = x[rows_of(chunk), :]
        h = jnp.maximum(dot(xc, wf[...]), 0.0).astype(BF16)
        hid[rows_of(chunk), :] = h
        f = (xc.astype(F32) + dot(h, ws[...])).astype(BF16)
        feat[rows_of(chunk), :] = f
        part = jnp.sum(f.astype(F32).reshape(SIZES[chunk] // IMG, IMG, C), axis=0)
        if chunk == 0:
            pooled[...] = part
        else:
            pooled[...] += part

    def rebuild(chunk):
        recon[rows_of(chunk), :] = dot(feat[rows_of(chunk), :], wp[...])

    def assemble(chunk):
        q = SIZES[chunk] // 4
        base = STARTS[chunk] * 3 // 4
        cut = lax.broadcasted_iota(jnp.int32, (q, 128), 1)
        for tile in range(6):
            filler, sub = (6 if tile < 3 else 7), tile % 3
            columns = pl.ds(tile * 128, 128)
            blocks = [pat[tile, pl.ds(base + a * q, q), :].astype(F32) for a in range(3)]
            for a in range(3):
                extra = pltpu.roll(pat[filler, pl.ds(base + a * q, q), :].astype(F32), 96 - 32 * sub, 1)
                target[pl.ds(a * q, q), columns] = jnp.where(cut < 96, blocks[a], extra).astype(BF16)
            turned = [pltpu.roll(blocks[a], 32 * (a + 1), 1) for a in range(3)]
            extra = pat[filler, pl.ds(base + sub * q, q), :].astype(F32)
            last = jnp.where(cut < 64, jnp.where(cut < 32, turned[0], turned[1]), jnp.where(cut < 96, turned[2], extra))
            target[pl.ds(3 * q, q), columns] = last.astype(BF16)

    def decode_grad(chunk):
        stage3(chunk)
        assemble(chunk)
        size = SIZES[chunk]
        rg = ((recon[rows_of(chunk), :] - target[pl.ds(0, size), :].astype(F32)) * (1.0 / 224.0)).astype(BF16)
        part = dot_tn(feat[rows_of(chunk), :], rg)
        if chunk == 0:
            acc_d[...] = part
        else:
            acc_d[...] += part
        return rg

    def feature_grad(chunk, rg):
        size = SIZES[chunk]
        back = dot_nt(rg, wp[...]).reshape(size // IMG, IMG, C) + pgrad[...][None]
        fg = back.reshape(size, C).astype(BF16)
        h = hid[rows_of(chunk), :]
        hg = jnp.where(h > 0, dot_nt(fg, ws[...]), 0.0).astype(BF16)
        return fg, hg

    def module_grads(chunk, fg, hg):
        part_s = dot_tn(hid[rows_of(chunk), :], fg)
        part_f = dot_tn(x[rows_of(chunk), :], hg)
        if chunk == 0:
            acc_s[...] = part_s
            acc_f[...] = part_f
        else:
            acc_s[...] += part_s
            acc_f[...] += part_f

    def spread(kind, src, dst):
        def one(k, _):
            peer = lax.rem(me_d + k, DP)
            rcopy(src(peer), dst, dsend.at[kind, peer], drecv.at[kind, me_d], {"dp": peer}).start()
            return 0

        lax.fori_loop(1, DP, one, 0)

    def collect(kind, slot):
        def one(k, _):
            peer = lax.rem(me_d + k, DP)
            rcopy(slot(peer), slot(peer), dsend.at[kind, peer], drecv.at[kind, peer], {"dp": peer}).wait_recv()
            return 0

        lax.fori_loop(1, DP, one, 0)

    loads[0].wait()
    for chunk in range(CHUNKS):
        pack(chunk)
    loads[1].wait()
    loads[2].wait()
    forward(0)
    pl.semaphore_wait(barrier, 3 + DP - 1)
    own_x(0)
    own_y(0)
    own_y(1)
    forward(1)
    forward(2)
    forward(3)

    loads[7].wait()
    pool_b = (pooled[...] * (1.0 / PIX)).astype(BF16)
    aux_out = jnp.maximum(dot(pool_b, wa[...]), 0.0).astype(BF16)
    auxall[me_d] = aux_out
    spread(0, lambda peer: auxall.at[me_d], auxall.at[me_d])
    for block in range(8):
        poolb[block] = pool_b[:, 128 * block:128 * (block + 1)]
    poolall[me_d] = poolb[chip]
    own_x(1)

    loads[8].wait()
    source = lax.broadcasted_iota(jnp.int32, (PATCH, PATCH), 0)
    place = lax.broadcasted_iota(jnp.int32, (PATCH, PATCH), 1)
    tile, lane = place >> 7, place & 127
    late = (tile >= 3).astype(jnp.int32)
    origin = jnp.where(
        lane < SLICE, SLICE * tile + lane, 6 * SLICE + SLICE * late + 32 * (tile - 3 * late) + lane - SLICE
    )
    wp[...] = dot(wd[...], (source == origin).astype(F32).astype(BF16)).astype(BF16)
    stage1(0)
    own_y(2)
    rebuild(0)
    rebuild(1)

    loads[9].wait()
    collect(0, lambda peer: auxall.at[peer])
    every = auxall[...].reshape(DP * IMG, HEAD)
    score = dot_nt(wc[...], every)
    logits[...] = score
    top = jnp.max(score, axis=0, keepdims=True)
    total = jnp.sum(jnp.exp(score - top), axis=0, keepdims=True)
    column = lax.broadcasted_iota(jnp.int32, (1, DP * IMG), 1)
    line = jnp.zeros((1, DP * IMG), F32)
    for image in range(IMG):
        line = jnp.where(column == me_d * IMG + image, labels[image].astype(F32), line)
    stats[me_d] = jnp.concatenate([top, total, line, jnp.zeros((5, DP * IMG), F32)], axis=0)
    spread(2, lambda peer: stats.at[me_d], stats.at[me_d])
    own_x(3)
    rebuild(2)
    rebuild(3)
    stage2(0)
    stage1(1)

    collect(2, lambda peer: stats.at[peer])
    table = stats[...]
    high = jnp.max(table[:, 0, :], axis=0, keepdims=True)
    denominator = jnp.sum(table[:, 1, :] * jnp.exp(table[:, 0, :] - high), axis=0, keepdims=True)
    label = jnp.sum(table[:, 2, :], axis=0, keepdims=True).astype(jnp.int32)
    prob = jnp.exp(logits[...] - high) / denominator
    number = lax.broadcasted_iota(jnp.int32, (CSHARD, DP * IMG), 0) + me_d * CSHARD
    lg = ((prob - (number == label).astype(F32)) * 0.0625).astype(BF16)
    backs[...] = dot_tn(lg, wc[...]).astype(BF16).reshape(DP, IMG, HEAD)
    spread(3, lambda peer: backs.at[peer], backr.at[me_d])
    backr[me_d] = backs[me_d]
    lgs[...] = lg
    auxout[...] = every
    own_x(2)
    stage1(2)
    own_y(3)
    rg = decode_grad(0)

    collect(3, lambda peer: backr.at[peer])
    aux_grad = jnp.where(auxall[me_d] > 0, jnp.sum(backr[...].astype(F32), axis=0), 0.0).astype(BF16)
    agall[me_d] = aux_grad
    pgrad[...] = dot_nt(aux_grad, wa[...]) * (1.0 / PIX)
    fg, hg = feature_grad(0, rg)
    stage2(1)
    stage1_across(3)
    module_grads(0, fg, hg)
    stage2(2)
    spread(4, lambda peer: agall.at[me_d], agall.at[me_d])
    spread(1, lambda peer: poolb.at[peer // 2], poolall.at[me_d])
    stage1_along(3)
    rg_first = decode_grad(1)
    stage2(3)
    rg_before = decode_grad(2)

    def pair(kind, mine, theirs):
        return rcopy(mine.at[1 - core], theirs, csend.at[kind], crecv.at[kind], {"dp": me_d + 1 - 2 * core})

    def split(acc, out, rows):
        whole = acc[...].astype(BF16).reshape(8, 2, rows, acc.shape[1])
        out[0] = whole[:, 0]
        out[1] = whole[:, 1]

    def chip_sum(kind, mine, theirs, out, got):
        pair(kind, mine, theirs).wait_recv()
        out[...] = (mine[core].astype(F32) + theirs[...].astype(F32)).astype(BF16)

        def one(k, _):
            peer = lax.rem(chip + k, 8)
            rcopy(
                out.at[peer], got.at[chip], tsend.at[kind, peer], trecv.at[kind, chip], {"dp": 2 * peer + core}
            ).start()
            return 0

        lax.fori_loop(1, 8, one, 0)
        got[chip] = out[chip]

    def total_sum(kind, got):
        def one(k, _):
            peer = lax.rem(chip + k, 8)
            rcopy(
                got.at[peer], got.at[peer], tsend.at[kind, peer], trecv.at[kind, peer], {"dp": 2 * peer + core}
            ).wait_recv()
            return 0

        lax.fori_loop(1, 8, one, 0)
        return jnp.sum(got[...].astype(F32), axis=0)

    last = CHUNKS - 1
    rg = decode_grad(last)
    split(acc_d, pd, 64)
    pair(0, pd, qd).start()
    module_grads(1, *feature_grad(1, rg_first))
    chip_sum(0, pd, qd, td, rd)
    module_grads(2, *feature_grad(2, rg_before))
    module_grads(last, *feature_grad(last, rg))
    split(acc_f, pf, 64)
    pair(1, pf, qf).start()
    split(acc_s, ps, 16)
    pair(2, ps, qs).start()
    chip_sum(1, pf, qf, tf, rf)
    chip_sum(2, ps, qs, ts, rs)

    collect(1, lambda peer: poolall.at[peer])
    collect(4, lambda peer: agall.at[peer])
    sums = jnp.zeros((128, HEAD), F32)
    for group in range(DP):
        sums += dot_tn(poolall[group], agall[group]).astype(BF16).astype(F32)
    gaacc[...] = sums
    ga[0] = gaacc[pl.ds(pl.multiple_of(64 * core, 64), 64), :]
    gsum = total_sum(0, rd)
    for s in range(SEC):
        if s < 6:
            gd[0, :, SLICE * s:SLICE * (s + 1)] = gsum[:, 128 * s:128 * s + SLICE]
        else:
            for sub in range(3):
                begin = 128 * (3 * (s - 6) + sub) + SLICE
                gd[0, :, SLICE * s + 32 * sub:SLICE * s + 32 * (sub + 1)] = gsum[:, begin:begin + 32]
    gf[0] = total_sum(1, rf)
    gs[0] = total_sum(2, rs)

    for copy in started:
        copy.wait_send()
    for kind, mine, theirs in ((0, pd, qd), (1, pf, qf), (2, ps, qs)):
        pair(kind, mine, theirs).wait_send()

    def drain(k, _):
        peer = lax.rem(me_d + k, DP)
        for kind, src in (
            (0, auxall.at[me_d]), (1, poolb.at[0]), (2, stats.at[me_d]), (3, backs.at[peer]), (4, agall.at[me_d])
        ):
            rcopy(src, src, dsend.at[kind, peer], drecv.at[kind, peer], {"dp": peer}).wait_send()
        return 0

    lax.fori_loop(1, DP, drain, 0)

    def drain_chip(k, _):
        peer = lax.rem(chip + k, 8)
        for kind, src in ((0, td), (1, tf), (2, ts)):
            rcopy(
                src.at[peer], src.at[peer], tsend.at[kind, peer], trecv.at[kind, peer], {"dp": 2 * peer + core}
            ).wait_send()
        return 0

    lax.fori_loop(1, 8, drain_chip, 0)


def finish(gf, gs, gd, ga, lgs, auxout, of, os, od, oa, oc):
    for source, out in ((gf, of), (gs, os), (gd, od), (ga, oa)):
        out[...] = source[...]
    oc[0] = dot(lgs[...], auxout[...])


def local_step(acts, patches, labels, w_first, w_second, w_decode, w_aux, w_class):
    any_spec = pl.BlockSpec(memory_space=pl.ANY)
    vmem = pl.BlockSpec(memory_space=pltpu.VMEM)
    big = max(SIZES)
    shapes = [
        ((ROWS, C), BF16), ((ROWS, C), BF16), ((ROWS, BOT), BF16), ((SEC, PROWS, 128), BF16), ((ROWS, SLICE), BF16),
        ((C, BOT), BF16), ((BOT, C), BF16), ((C, PATCH), BF16), ((C, PATCH), BF16), ((C, HEAD), BF16),
        ((CSHARD, HEAD), BF16), ((ROWS, PATCH), F32),
        ((IMG, C), F32), ((8, IMG, 128), BF16), ((DP, IMG, HEAD), BF16), ((DP, IMG, 128), BF16),
        ((DP, 8, DP * IMG), F32), ((CSHARD, DP * IMG), F32), ((DP, IMG, HEAD), BF16), ((DP, IMG, HEAD), BF16),
        ((DP, IMG, HEAD), BF16), ((IMG, C), F32),
        ((big, PATCH), BF16), ((C, BOT), F32), ((BOT, C), F32), ((C, PATCH), F32), ((128, HEAD), F32),
        ((2, 8, 64, BOT), BF16), ((2, 8, 16, C), BF16), ((2, 8, 64, PATCH), BF16),
    ] + [((8, 64, BOT), BF16), ((8, 16, C), BF16), ((8, 64, PATCH), BF16)] * 3
    shapes_out = (
        jax.ShapeDtypeStruct((1, 64, BOT), F32), jax.ShapeDtypeStruct((1, 16, C), F32),
        jax.ShapeDtypeStruct((1, 64, PATCH), F32), jax.ShapeDtypeStruct((1, 64, HEAD), F32),
        jax.ShapeDtypeStruct((1, CSHARD, HEAD), F32),
    )
    results = pl.pallas_call(
        kernel,
        name="step",
        out_shape=shapes_out[:4] + (
            jax.ShapeDtypeStruct((CSHARD, DP * IMG), BF16), jax.ShapeDtypeStruct((DP * IMG, HEAD), BF16),
        ),
        in_specs=[any_spec, any_spec, pl.BlockSpec(memory_space=pltpu.SMEM)] + [any_spec] * 5,
        out_specs=[vmem] * 6,
        scratch_shapes=[pltpu.VMEM(shape, kind) for shape, kind in shapes] + [
            pltpu.SemaphoreType.DMA((10,)),
            pltpu.SemaphoreType.DMA((CHUNKS, 14)), pltpu.SemaphoreType.DMA((CHUNKS, 2, SEC)),
            pltpu.SemaphoreType.DMA((5, DP)), pltpu.SemaphoreType.DMA((5, DP)),
            pltpu.SemaphoreType.DMA((3,)), pltpu.SemaphoreType.DMA((3,)),
            pltpu.SemaphoreType.DMA((3, 8)), pltpu.SemaphoreType.DMA((3, 8)),
        ],
        compiler_params=pltpu.CompilerParams(
            collective_id=0, has_side_effects=True, vmem_limit_bytes=63 * 2**20
        ),
        cost_estimate=pl.CostEstimate(flops=25 * 10**9, bytes_accessed=16 * 10**6, transcendentals=400000),
    )(
        jnp.transpose(acts[0], (1, 0, 2)).reshape(ROWS, C),
        jnp.transpose(patches, (1, 0, 2)).reshape(ROWS, SLICE), labels,
        w_first, w_second, w_decode, w_aux, w_class,
    )
    return pl.pallas_call(
        finish,
        name="finish",
        out_shape=shapes_out,
        in_specs=[vmem] * 6,
        out_specs=[vmem] * 5,
    )(*results)


def solution(mesh):
    in_specs = (
        P("section", "dp", None, None),
        P("dp", None, "section"),
        P("dp"),
        P("section", None, None),
        P("section", None, None),
        P("section", None, None),
        P("section", None, None),
        P("section", "dp", None),
    )
    out_specs = (P("section", "dp", None),) * 5
    return jax.shard_map(local_step, mesh=mesh, in_specs=in_specs, out_specs=out_specs, check_vma=False)
```
